256 devices in a mesh: plane: 8 (over x, core), row: 32 (over z, y).
Axes of the slice: x: 4, y: 4, z: 8, core: 2. Of those that a mesh axis runs over, the one named last changes fastest.
Arguments:
- image: float32 [2, 2048, 2048], P(None, 'row'), may hold values from -6 to 6
- w_planes: float32 [8], P('plane'), may hold values from -200 to 200
- owner: int32 [8, 1024, 1], P('plane'), may hold values from 0 to 31; in each aligned block of 32 rows (0 to 31, 32 to 63, ..., all dimensions but the last counted through in order) at most 2 rows name the same one
- positions: int32 [8, 2, 2048, 256], P('plane', None, 'row'), may hold values from 0 to 7295
- weights: float32 [8, 2048, 256], P('plane', 'row'), may hold values from 0.2 to 2
- counts: int32 [8, 2048], P('plane', 'row'), may hold values from 64 to 256, as said below
Outputs:
- normal_image: float32 [2, 2048, 2048], P(None, 'row', 'plane')
The draws below stay inside these ranges and needn't reach their ends.
Inputs may be any that keep to these rules, and one draw needn't show every extreme that they name: In every plane the 32 tiles of one source index give no owner more than 2 of them; every owner is used somewhere. `counts`: slots that no tile fills are ignored; in every plane some slots have exactly 256.
All inputs are finite; a program needn't handle non-finite values.
Results may differ from the reference program's by a relative error of at most 0.0075.
Values may be sent and summed in bfloat16 or wider, within the bound.
A program may use at most 64 MiB of HBM per device.

```python
import math
import jax
import jax.numpy as jnp
import numpy as np
from jax import lax

G = 2048
TILE = 64
S = 8
OVER = 128
V = 256
PLANES = 8
TPD = 32
TILES = 1024
MOST = 2
SLOTS = 64
SALL = 2048
N_ROW = 32


def draw_counts(key, part):
    values = jax.random.randint(key, (PLANES, SALL), V // 4, V + 1)
    columns = jnp.arange(SALL, dtype=jnp.int32)[None, :]
    return jnp.where(columns % MOST == 0, V, values).astype(jnp.int32)


def touch_ends(drawn, own_key, low, high):
    shape = drawn.shape
    index_at = [jax.random.randint(jax.random.fold_in(own_key, axis), (), 0, shape[axis]) for axis in range(len(shape))]
    drawn = drawn.at[tuple(index_at)].set(low)
    longest = shape.index(max(shape))
    index_at[longest] = (index_at[longest] + 1) % shape[longest]
    return drawn.at[tuple(index_at)].set(high)


def steps_of(stream_key, shape, shards, least, top_value):
    gain, own = 1.0, jax.random.fold_in(stream_key, 6)
    for axis_at, blocks in shards:
        steps = jnp.exp(jax.random.uniform(jax.random.fold_in(own, axis_at), (blocks,), jnp.float32, least / len(shards), top_value / len(shards)))
        gain = gain * jnp.repeat(steps, shape[axis_at] // blocks).reshape([-1 if axis == axis_at else 1 for axis in range(len(shape))])
    return gain


def deal_out(stream_key, own, number, rows, amount, top, limit, skew):
    sequence = jax.random.permutation(stream_key, amount)
    packed, ordinary = shares(amount, rows * top, limit, skew, True), shares(amount, rows * top, limit, skew, False)
    places = jnp.arange(amount)

    def named(sizes, rotation):
        used = int((sizes > 0).sum())
        fixed = max(1, used // 4)
        moved = fixed + (places - fixed + rotation * (used - fixed)) % max(1, amount - fixed)
        return jnp.zeros((amount,), jnp.int32).at[sequence[jnp.where(places < fixed, places, moved)]].set(jnp.asarray(sizes, jnp.int32))

    sizes = jnp.where(number % 4 == 0, named(packed, number // 4), named(ordinary, number - number // 4 - 1))
    mixed = jax.random.permutation(jax.random.fold_in(own, 3), amount)
    donor, taker = mixed[0:amount // 2 * 2:2], mixed[1:amount // 2 * 2:2]
    margin = jnp.minimum(sizes[donor] - 1, limit - sizes[taker]) // 2
    margin = jnp.where((donor == sequence[0]) | (taker == sequence[0]) | (sizes[taker] == 0), 0, jnp.maximum(margin, 0))
    moved = jax.random.randint(jax.random.fold_in(own, 4), (amount // 2,), 0, 1 << 20) % (margin + 1)
    sizes = sizes.at[donor].add(-moved).at[taker].add(moved)
    items = jnp.searchsorted(jnp.cumsum(sizes), jnp.arange(rows * top), side="right").astype(jnp.int32)
    table = items.reshape(top, rows).T
    table = table[jax.random.permutation(jax.random.fold_in(own, 1), rows)]
    rotation = jax.random.randint(jax.random.fold_in(own, 2), (rows, 1), 0, top)
    return jnp.take_along_axis(table, (jnp.arange(top)[None, :] + rotation) % top, axis=1)


def shares(count, total, bound, skew, full):
    weights = [(1 << 20) // math.isqrt(rank ** skew) + 1 for rank in range(1, count + 1)]
    largest = bound if full else min(bound, max(-(-total // count), total * weights[0] // sum(weights)))
    least = 1 if total - largest >= count - 1 else 0
    given, rest = [largest] + [least] * (count - 1), total - largest - least * (count - 1)
    while rest > 0:
        free = [i for i in range(1, count) if given[i] < largest] or [i for i in range(1, count) if given[i] < bound]
        pool, left = sum([weights[i] for i in free]), rest
        for i in free:
            addition = min(bound - given[i], max(1, left * weights[i] // pool), rest)
            given[i] = given[i] + addition
            rest = rest - addition
    return np.array(given)


def normal_values(key, shape, deviation, bound, split=(), held_as=jnp.bfloat16):
    entries = deviation * jax.random.normal(key, shape, jnp.float32)
    if split:
        entries = entries * steps_of(key, shape, split, -0.22, 0.18)
    return jnp.clip(entries, -bound, bound).astype(held_as)


def setup_inputs(seed: int = 0) -> dict:
    keys = jax.random.split(jax.random.key(seed), 7)
    image = normal_values(keys[0], (2, G, G), 1.0, 6.0, ((1, 32),), jnp.float32)
    w_planes = jnp.clip(jax.random.uniform(keys[1], (PLANES,), jnp.float32, -200.0, 200.0) * steps_of(keys[1], (PLANES,), ((0, 8),), -0.4, 0.0), -200.0, 200.0)
    owner_keys = jax.random.split(jax.random.fold_in(keys[2], 1), PLANES * TILES // TPD)
    owner_turns = jax.random.permutation(jax.random.fold_in(keys[2], 3), PLANES * TILES // TPD)
    owner = jax.vmap(lambda own, number: deal_out(jax.random.fold_in(keys[2], 2), own, number, TPD, N_ROW, 1, MOST, 2))(owner_keys, owner_turns).reshape((PLANES, TILES, 1))
    positions = touch_ends(jax.random.randint(keys[3], (PLANES, 2, SALL, V), 0, (TILE - S + 1) * OVER), jax.random.fold_in(keys[3], 1), 0, ((TILE - S + 1) * OVER) - 1).astype(jnp.int32)
    weights = jnp.clip(jnp.exp(math.log(2.0) - 2.3025851 * jax.random.uniform(keys[4], (PLANES, SALL, V), jnp.float32) ** steps_of(keys[4], (PLANES, SALL, V), ((0, 8), (1, 32)), -0.2, 0.2)), 0.2, 2.0)
    counts = draw_counts(jax.random.fold_in(keys[6], 71), 0)
    return dict(image=image, w_planes=w_planes, owner=owner, positions=positions, weights=weights, counts=counts)


KERNEL_BETA = 64.0
FIELD_SPAN = 0.7

def kernel_taps(position):
    corner = position // OVER
    fraction = (position % OVER).astype(jnp.float32) / OVER
    offsets = jnp.arange(S, dtype=jnp.int32).astype(jnp.float32)
    distance = offsets[None, :] - float(S // 2 - 1) - fraction[:, None]
    scaled = distance * (2.0 / S)
    rounded = jnp.exp(-KERNEL_BETA * scaled * scaled).astype(jnp.bfloat16)
    return (corner, lax.optimization_barrier(rounded).astype(jnp.float32))

def grid_tile(operands):
    tile_block, position, weight, valid = operands
    corner_u, taps_u = kernel_taps(position[0])
    corner_v, taps_v = kernel_taps(position[1])
    reach = jnp.arange(S, dtype=jnp.int32)
    row_index = (corner_u[:, None] + reach[None, :])[:, :, None]
    col_index = (corner_v[:, None] + reach[None, :])[:, None, :]
    patch = tile_block.astype(jnp.float32)[:, row_index, col_index]
    predicted = jnp.einsum('ka,ckab,kb->ck', taps_u, patch, taps_v)
    usable = jnp.arange(V, dtype=jnp.int32) < valid
    weighted = predicted * jnp.where(usable, weight, 0.0)[None, :]
    spread = (taps_v[None, :, :] * weighted[:, :, None]).astype(jnp.bfloat16)
    spread = lax.optimization_barrier(spread).astype(jnp.float32)
    contrib = taps_u[None, :, :, None] * spread[:, :, None, :]
    gridded = jnp.zeros((2, TILE, TILE), jnp.float32).at[:, row_index, col_index].add(contrib)
    return gridded.astype(jnp.bfloat16)

def reference(image, w_planes, owner, positions, weights, counts):
    extent = image.shape[1]
    across = extent // TILE
    per_device = extent // (TILE * N_ROW)
    tiles_each = across * per_device
    axis_values = (jnp.arange(extent, dtype=jnp.int32) - extent // 2).astype(jnp.float32) * (FIELD_SPAN / extent)
    elevation = jnp.sqrt(1.0 - axis_values[:, None] * axis_values[:, None] - axis_values[None, :] * axis_values[None, :]) - 1.0
    total = jnp.zeros((2, extent, extent), jnp.float32)
    sources = jnp.arange(N_ROW, dtype=jnp.int32)
    for plane_index in range(PLANES):
        phase_angle = 2.0 * math.pi * w_planes[plane_index] * elevation
        cosine = jnp.cos(phase_angle)
        sine_part = jnp.sin(phase_angle)
        screened_real = image[0] * cosine + image[1] * sine_part
        screened_imag = image[1] * cosine - image[0] * sine_part
        spectrum = jnp.fft.fft2(screened_real + 1j * screened_imag, norm='ortho')
        grid = jnp.stack([jnp.real(spectrum), jnp.imag(spectrum)]).astype(jnp.bfloat16)
        tile_stack = grid.reshape(2, across, TILE, N_ROW, per_device, TILE).transpose(3, 1, 4, 0, 2, 5).reshape(TILES, 2, TILE, TILE)
        owners = owner[plane_index, :, 0].reshape(N_ROW, tiles_each)
        onehot = (owners[:, :, None] == sources[None, None, :]).astype(jnp.int32)
        ranked = lax.optimization_barrier(jnp.sum((jnp.cumsum(onehot, axis=1) - onehot) * onehot, axis=2))
        slot_index = (owners * SLOTS + sources[:, None] * MOST + ranked).reshape(-1).astype(jnp.int32)
        tile_position = jnp.take(positions[plane_index], slot_index, axis=1).transpose(1, 0, 2)
        tile_weight = jnp.take(weights[plane_index], slot_index, axis=0)
        tile_count = jnp.take(counts[plane_index], slot_index, axis=0)
        gridded = lax.map(grid_tile, (tile_stack, tile_position, tile_weight, tile_count))
        gridded_grid = gridded.reshape(N_ROW, across, per_device, 2, TILE, TILE).transpose(3, 1, 4, 0, 2, 5).reshape(2, extent, extent)
        field = jnp.fft.ifft2(gridded_grid[0].astype(jnp.float32) + 1j * gridded_grid[1].astype(jnp.float32), norm='ortho')
        final_real = jnp.real(field).astype(jnp.float32)
        final_imag = jnp.imag(field).astype(jnp.float32)
        total = total + jnp.stack([final_real * cosine - final_imag * sine_part, final_real * sine_part + final_imag * cosine])
    return total
```

```python
import functools

import jax
import jax.numpy as jnp
import ml_dtypes
import numpy as np
from jax import lax
from jax.experimental import pallas as pl
from jax.experimental.pallas import tpu as pltpu
from jax.sharding import PartitionSpec as P

TILE = 64
S = 8
OVER = 128
V = 256
FIELD_SPAN = 0.7
EXTENT = 2048
ROWS = 32
PLANES = 8
SCALE = 1.0 / 2048.0
TAP_RATE = -4.0 * 1.4426950408889634
MESH = pl.DeviceIdType.MESH
F32 = jnp.float32
BF16 = jnp.bfloat16
ROOT = 0.7071067811865476
SIN_POLY = (6.283184916495429, -41.34158923268831, 81.59994332977428, -76.61447253115396, 41.342882354135696, -12.471243534350362)
COS_POLY = (0.9999999890590228, -19.739204499453827, 64.9391174598908, -85.45013953079768, 60.16763095026347, -25.967599245923736, 6.52865815775625)


def host_tables():
    index = np.arange(256)
    angle = 2.0 * np.pi / 256.0 * (index[:, None] * index[None, :] % 256)
    cosine, sine = np.cos(angle), np.sin(angle)
    table = np.block([[cosine, sine], [-sine, cosine]]).astype(ml_dtypes.bfloat16)
    turn = 2.0 * np.pi / 2048.0 * (np.arange(8)[:, None] * index[None, :])
    return table, np.stack([np.cos(turn), np.sin(turn)]).astype(np.float32)


def dft4(re, im):
    ar, ai, br, bi = re[0] + re[2], im[0] + im[2], re[0] - re[2], im[0] - im[2]
    cr, ci, dr, di = re[1] + re[3], im[1] + im[3], re[1] - re[3], im[1] - im[3]
    return [ar + cr, br - di, ar - cr, br + di], [ai + ci, bi + dr, ai - ci, bi - dr]


def dft8(re, im):
    er, ei = dft4(re[0::2], im[0::2])
    od, oi = dft4(re[1::2], im[1::2])
    tr = [od[0], (od[1] - oi[1]) * ROOT, -oi[2], (od[3] + oi[3]) * -ROOT]
    ti = [oi[0], (od[1] + oi[1]) * ROOT, od[2], (od[3] - oi[3]) * ROOT]
    return [er[k] + tr[k] for k in range(4)] + [er[k] - tr[k] for k in range(4)], [
        ei[k] + ti[k] for k in range(4)
    ] + [ei[k] - ti[k] for k in range(4)]


def swap_halves(value):
    return pltpu.roll(value, 64, 1)


def screen_of(turns):
    part = turns - jnp.round(turns)
    square = part * part
    sine = jnp.full_like(part, SIN_POLY[-1])
    for term in SIN_POLY[-2::-1]:
        sine = sine * square + term
    cosine = jnp.full_like(part, COS_POLY[-1])
    for term in COS_POLY[-2::-1]:
        cosine = cosine * square + term
    return cosine * SCALE, sine * part * SCALE


def chunk_screen(w, row_start, col_start):
    spacing = FIELD_SPAN / EXTENT
    rows = lax.broadcasted_iota(jnp.int32, (16, 128), 0) + (row_start - EXTENT // 2)
    cols = lax.broadcasted_iota(jnp.int32, (16, 128), 1) + (col_start - EXTENT // 2)
    rows = rows.astype(F32) * spacing
    cols = cols.astype(F32) * spacing
    elevation = jnp.sqrt(1.0 - rows * rows - cols * cols) - 1.0
    return screen_of(w * elevation)


def spread_out(load, twiddle, stacked):
    def step(block, carry):
        rows = pl.ds(pl.multiple_of(block * 16, 16), 16)
        for half in range(2):
            pairs = load(block, rows, half)
            re, im = dft8([pair[0] for pair in pairs], [pair[1] for pair in pairs])
            lanes = slice(128 * half, 128 * half + 128)
            other = slice(256 + 128 * half, 384 + 128 * half)
            for q in range(8):
                if q == 0:
                    real, imag = re[0], im[0]
                else:
                    cosine, sine = twiddle[0, q : q + 1, lanes], twiddle[1, q : q + 1, lanes]
                    real, imag = re[q] * cosine - im[q] * sine, re[q] * sine + im[q] * cosine
                stacked[q, rows, lanes] = real.astype(BF16)
                stacked[q, rows, other] = imag.astype(BF16)
        return carry

    lax.fori_loop(0, 4, step, 0)


def turn_blocks(stacked, table, blocks):
    matrix = table[...]
    for pair in range(4):
        left = stacked[2 * pair : 2 * pair + 2].reshape(128, 512)
        out = jnp.dot(left, matrix, preferred_element_type=F32)
        for half in range(2):
            real, imag = slice(128 * half, 128 * half + 128), slice(256 + 128 * half, 384 + 128 * half)
            turned = []
            for item in range(2):
                rows = slice(64 * item, 64 * item + 64)
                square = jnp.concatenate([out[rows, real], out[rows, imag]], axis=0)
                turned.append(jnp.transpose(square).reshape(16, 8, 128))
            both = jnp.concatenate(turned, axis=1).astype(BF16)
            blocks[16 * half : 16 * half + 16, 16 * pair : 16 * pair + 16, :] = both


def gather_blocks(blocks, table, twiddle, middle):
    matrix = table[...]
    for pair in range(4):
        rows = blocks[:, 16 * pair : 16 * pair + 16, :].astype(F32)
        for item in range(2):
            q = 2 * pair + item
            flat = rows[:, 8 * item : 8 * item + 8, :].reshape(256, 128)
            low = jnp.transpose(flat[0:128]).astype(BF16)
            high = jnp.transpose(flat[128:256]).astype(BF16)
            left = jnp.concatenate([low[0:64], high[0:64], low[64:128], high[64:128]], axis=1)
            out = jnp.dot(left, matrix, preferred_element_type=F32)
            real, imag = out[:, 0:256], out[:, 256:512]
            if q:
                cosine, sine = twiddle[0, q : q + 1, :], twiddle[1, q : q + 1, :]
                real, imag = real * cosine - imag * sine, real * sine + imag * cosine
            middle[q, :, 0:256] = real
            middle[q, :, 256:512] = imag


def gather_last(middle, emit):
    def step(block, carry):
        rows = pl.ds(pl.multiple_of(block * 16, 16), 16)
        for half in range(2):
            lanes = slice(128 * half, 128 * half + 128)
            other = slice(256 + 128 * half, 384 + 128 * half)
            re, im = dft8([middle[q, rows, lanes] for q in range(8)], [middle[q, rows, other] for q in range(8)])
            emit(block, rows, half, re, im)
        return carry

    lax.fori_loop(0, 4, step, 0)


def low_lanes():
    return lax.broadcasted_iota(jnp.int32, (16, 128), 1) < 64


def load_received(blocks):
    def load(block, rows, half):
        low = low_lanes()
        pairs = []
        for a in range(8):
            first = blocks[4 * a + 2 * half, rows, :].astype(F32)
            second = blocks[4 * a + 2 * half + 1, rows, :].astype(F32)
            pairs.append(
                (jnp.where(low, first, swap_halves(second)), jnp.where(low, swap_halves(first), second))
            )
        return pairs

    return load


def emit_blocks(blocks):
    def emit(block, rows, half, re, im):
        low = low_lanes()
        for a in range(8):
            blocks[4 * a + 2 * half, rows, :] = jnp.where(low, re[a], swap_halves(im[a])).astype(BF16)
            blocks[4 * a + 2 * half + 1, rows, :] = jnp.where(low, swap_halves(re[a]), im[a]).astype(BF16)

    return emit


def taps_of(position, places):
    distance = places - position
    inside = (distance > -4.0) & (distance <= 4.0)
    return jnp.where(inside, jnp.exp2(distance * distance * TAP_RATE), 0.0)


def place_index():
    place = lax.broadcasted_iota(jnp.int32, (TILE, V), 0)
    return (place // 8 + 8 * lax.rem(place, 8) - 3).astype(F32)


def grid_tile(tile, packed, weight, places):
    u_part = packed // 8192
    u_place = u_part.astype(F32) * (1.0 / OVER)
    v_place = (packed - u_part * 8192).astype(F32) * (1.0 / OVER)
    taps_u = taps_of(u_place, places).astype(BF16)
    taps_v = taps_of(v_place, places).astype(BF16).astype(F32)
    partial = lax.dot_general(tile, taps_u, (((0,), (0,)), ((), ())), preferred_element_type=F32)
    real = jnp.sum(partial[0:64] * taps_v, axis=0, keepdims=True) * weight
    imag = jnp.sum(partial[64:128] * taps_v, axis=0, keepdims=True) * -weight
    spread = jnp.concatenate([taps_v * real, taps_v * imag], axis=0).astype(BF16)
    return lax.dot_general(taps_u, spread, (((1,), (1,)), ((), ())), preferred_element_type=F32).astype(BF16)


def exchange_start(source, target, send, recv, me):
    def step(offset, carry):
        peer = lax.rem(me + offset, ROWS)
        pltpu.make_async_remote_copy(
            source.at[peer], target.at[me], send.at[peer], recv.at[me], device_id={"row": peer}, device_id_type=MESH
        ).start()
        return carry

    lax.fori_loop(1, ROWS, step, 0)


def exchange_wait(source, target, send, recv, me):
    def step(offset, carry):
        peer = lax.rem(me + offset, ROWS)
        copy = pltpu.make_async_remote_copy(
            source.at[peer], target.at[peer], send.at[peer], recv.at[peer], device_id={"row": peer}, device_id_type=MESH
        )
        copy.wait_send()
        copy.wait_recv()
        return carry

    lax.fori_loop(1, ROWS, step, 0)


def greet(axis, size, me, barrier):
    def step(offset, carry):
        pl.semaphore_signal(
            barrier, inc=1, device_id={axis: lax.rem(me + offset, size)}, device_id_type=MESH
        )
        return carry

    lax.fori_loop(1, size, step, 0)


def first_kernel(
    w_ref, image, packed, weight, table, twiddle, got, got_packed, got_weight, stacked, blocks, send, recv
):
    me = lax.axis_index("row")
    barrier = pltpu.get_barrier_semaphore()
    greet("row", ROWS, me, barrier)
    w = w_ref[0]

    def load(block, rows, half):
        pairs = []
        for a in range(8):
            col = 256 * a + 128 * half
            cosine, sine = chunk_screen(w, me * 64 + block * 16, col)
            real, imag = image[0, rows, col : col + 128], image[1, rows, col : col + 128]
            pairs.append((real * cosine + imag * sine, real * sine - imag * cosine))
        return pairs

    pl.semaphore_wait(barrier, ROWS - 1)
    exchange_start(packed, got_packed, send.at[0], recv.at[0], me)
    exchange_start(weight, got_weight, send.at[1], recv.at[1], me)
    got_packed[me] = packed[me]
    got_weight[me] = weight[me]
    spread_out(load, twiddle, stacked)
    turn_blocks(stacked, table, blocks)
    exchange_start(blocks, got, send.at[2], recv.at[2], me)
    got[me] = blocks[me]
    exchange_wait(packed, got_packed, send.at[0], recv.at[0], me)
    exchange_wait(weight, got_weight, send.at[1], recv.at[1], me)
    exchange_wait(blocks, got, send.at[2], recv.at[2], me)


def second_kernel(
    owner, got, packed, weight, table, twiddle, out, stacked, tiles, gridded, middle, slots, seen
):
    me = lax.axis_index("row")
    for place in range(ROWS):
        seen[place] = 0

    def rank(item, carry):
        name = owner[me * ROWS + item]
        before = seen[name]
        slots[item] = name * 2 + before
        seen[name] = before + 1
        return carry

    lax.fori_loop(0, ROWS, rank, 0)
    spread_out(load_received(got), twiddle, stacked)
    turn_blocks(stacked, table, tiles)
    places = place_index()

    def step(item, carry):
        slot = slots[item]
        name, second = slot // 2, lax.rem(slot, 2)
        gridded[item] = grid_tile(
            tiles[item], packed[name, pl.ds(second, 1), :], weight[name, pl.ds(second, 1), :], places
        )
        return carry

    lax.fori_loop(0, ROWS, step, 0, unroll=2)
    gather_blocks(gridded, table, twiddle, middle)
    gather_last(middle, emit_blocks(out))


def third_kernel(
    w_ref, blocks, table, twiddle, out, got, middle, screen, terms, others, send, recv, plane_send, plane_recv
):
    me = lax.axis_index("row")
    plane = lax.axis_index("plane")
    barrier = pltpu.get_barrier_semaphore()
    greet("row", ROWS, me, barrier)
    greet("plane", PLANES, plane, barrier)
    pl.semaphore_wait(barrier, ROWS + PLANES - 2)
    exchange_start(blocks, got, send, recv, me)
    got[me] = blocks[me]
    w = w_ref[0]

    def prepare(block, carry):
        rows = pl.ds(pl.multiple_of(block * 16, 16), 16)
        for piece in range(16):
            lanes = slice(128 * piece, 128 * piece + 128)
            cosine, sine = chunk_screen(w, me * 64 + block * 16, 128 * piece)
            screen[0, rows, lanes] = cosine
            screen[1, rows, lanes] = sine
        return carry

    lax.fori_loop(0, 4, prepare, 0)
    exchange_wait(blocks, got, send, recv, me)
    gather_blocks(got, table, twiddle, middle)

    def emit(block, rows, half, re, im):
        for a in range(8):
            lanes = slice(128 * half, 128 * half + 128)
            full = slice(256 * a + 128 * half, 256 * a + 128 * half + 128)
            cosine, sine = screen[0, rows, full], screen[1, rows, full]
            terms[a, 0, rows, lanes] = (re[a] * cosine - im[a] * sine).astype(BF16)
            terms[a, 1, rows, lanes] = (re[a] * sine + im[a] * cosine).astype(BF16)

    gather_last(middle, emit)
    for offset in range(1, PLANES):
        peer = lax.rem(plane + offset, PLANES)
        pltpu.make_async_remote_copy(
            terms.at[peer],
            others.at[plane],
            plane_send.at[peer],
            plane_recv.at[plane],
            device_id={"plane": peer},
            device_id_type=MESH,
        ).start()
    out[...] = terms[plane].astype(F32)
    for offset in range(1, PLANES):
        peer = lax.rem(plane + offset, PLANES)
        copy = pltpu.make_async_remote_copy(
            terms.at[peer],
            others.at[peer],
            plane_send.at[peer],
            plane_recv.at[peer],
            device_id={"plane": peer},
            device_id_type=MESH,
        )
        copy.wait_send()
        copy.wait_recv()
        out[...] += others[peer].astype(F32)


def local(image, w_planes, owner, positions, weights, counts):
    table, twiddle = host_tables()
    table, twiddle = jnp.asarray(table), jnp.asarray(twiddle)
    vmem = pl.BlockSpec(memory_space=pltpu.VMEM)
    smem = pl.BlockSpec(memory_space=pltpu.SMEM)
    packed = (positions[0, 0] * 8192 + positions[0, 1]).reshape(ROWS, 2, V)
    usable = jnp.arange(V, dtype=jnp.int32)[None, :] < counts[0][:, None]
    weight = jnp.where(usable, weights[0], 0.0).reshape(ROWS, 2, V)
    dma = pltpu.SemaphoreType.DMA
    block_shape = jax.ShapeDtypeStruct((ROWS, TILE, 128), BF16)
    got, packed, weight = pl.pallas_call(
        first_kernel,
        out_shape=(
            block_shape,
            jax.ShapeDtypeStruct((ROWS, 2, V), jnp.int32),
            jax.ShapeDtypeStruct((ROWS, 2, V), F32),
        ),
        in_specs=[smem] + [vmem] * 5,
        out_specs=(vmem, vmem, vmem),
        scratch_shapes=[
            pltpu.VMEM((8, 64, 512), BF16),
            pltpu.VMEM((ROWS, TILE, 128), BF16),
            dma((3, ROWS)),
            dma((3, ROWS)),
        ],
        compiler_params=pltpu.CompilerParams(collective_id=0, has_side_effects=True),
        name="first",
    )(w_planes, image, packed, weight, table, twiddle)
    blocks = pl.pallas_call(
        second_kernel,
        out_shape=block_shape,
        in_specs=[smem] + [vmem] * 5,
        out_specs=vmem,
        scratch_shapes=[
            pltpu.VMEM((8, 64, 512), BF16),
            pltpu.VMEM((ROWS, TILE, 128), BF16),
            pltpu.VMEM((ROWS, TILE, 128), BF16),
            pltpu.VMEM((8, 64, 512), F32),
            pltpu.SMEM((ROWS,), jnp.int32),
            pltpu.SMEM((ROWS,), jnp.int32),
        ],
        name="second",
    )(owner.reshape(-1), got, packed, weight, table, twiddle)
    return pl.pallas_call(
        third_kernel,
        out_shape=jax.ShapeDtypeStruct((2, 64, 256), F32),
        in_specs=[smem] + [vmem] * 3,
        out_specs=vmem,
        scratch_shapes=[
            pltpu.VMEM((ROWS, TILE, 128), BF16),
            pltpu.VMEM((8, 64, 512), F32),
            pltpu.VMEM((2, 64, EXTENT), F32),
            pltpu.VMEM((PLANES, 2, 64, 256), BF16),
            pltpu.VMEM((PLANES, 2, 64, 256), BF16),
            dma((ROWS,)),
            dma((ROWS,)),
            dma((PLANES,)),
            dma((PLANES,)),
        ],
        compiler_params=pltpu.CompilerParams(collective_id=1, has_side_effects=True),
        name="third",
    )(w_planes, blocks, table, twiddle)


def solution(mesh):
    in_specs = (
        P(None, "row", None),
        P("plane"),
        P("plane", None, None),
        P("plane", None, "row", None),
        P("plane", "row", None),
        P("plane", "row"),
    )
    out_specs = P(None, "row", "plane")
    return jax.shard_map(local, mesh=mesh, in_specs=in_specs, out_specs=out_specs, check_vma=False)
```

```python
import functools

import jax
import jax.numpy as jnp
import ml_dtypes
import numpy as np
from jax import lax
from jax.experimental import pallas as pl
from jax.experimental.pallas import tpu as pltpu
from jax.sharding import PartitionSpec as P

TILE = 64
S = 8
OVER = 128
V = 256
FIELD_SPAN = 0.7
EXTENT = 2048
ROWS = 32
PLANES = 8
SCALE = 1.0 / 2048.0
TAP_RATE = -4.0 * 1.4426950408889634
MESH = pl.DeviceIdType.MESH
F32 = jnp.float32
BF16 = jnp.bfloat16
ROOT = 0.7071067811865476
SIN_POLY = (6.283184916495429, -41.34158923268831, 81.59994332977428, -76.61447253115396, 41.342882354135696, -12.471243534350362)
COS_POLY = (0.9999999890590228, -19.739204499453827, 64.9391174598908, -85.45013953079768, 60.16763095026347, -25.967599245923736, 6.52865815775625)


def host_tables():
    index = np.arange(256)
    angle = 2.0 * np.pi / 256.0 * (index[:, None] * index[None, :] % 256)
    cosine, sine = np.cos(angle), np.sin(angle)
    table = np.block([[cosine, sine], [-sine, cosine]]).astype(ml_dtypes.bfloat16)
    turn = 2.0 * np.pi / 2048.0 * (np.arange(8)[:, None] * index[None, :])
    return table, np.stack([np.cos(turn), np.sin(turn)]).astype(np.float32)


def dft4(re, im):
    ar, ai, br, bi = re[0] + re[2], im[0] + im[2], re[0] - re[2], im[0] - im[2]
    cr, ci, dr, di = re[1] + re[3], im[1] + im[3], re[1] - re[3], im[1] - im[3]
    return [ar + cr, br - di, ar - cr, br + di], [ai + ci, bi + dr, ai - ci, bi - dr]


def dft8(re, im):
    er, ei = dft4(re[0::2], im[0::2])
    od, oi = dft4(re[1::2], im[1::2])
    tr = [od[0], (od[1] - oi[1]) * ROOT, -oi[2], (od[3] + oi[3]) * -ROOT]
    ti = [oi[0], (od[1] + oi[1]) * ROOT, od[2], (od[3] - oi[3]) * ROOT]
    return [er[k] + tr[k] for k in range(4)] + [er[k] - tr[k] for k in range(4)], [
        ei[k] + ti[k] for k in range(4)
    ] + [ei[k] - ti[k] for k in range(4)]


def swap_halves(value):
    return pltpu.roll(value, 64, 1)


def screen_of(turns):
    part = turns - jnp.round(turns)
    square = part * part
    sine = jnp.full_like(part, SIN_POLY[-1])
    for term in SIN_POLY[-2::-1]:
        sine = sine * square + term
    cosine = jnp.full_like(part, COS_POLY[-1])
    for term in COS_POLY[-2::-1]:
        cosine = cosine * square + term
    return cosine * SCALE, sine * part * SCALE


def chunk_screen(w, row_start, col_start):
    spacing = FIELD_SPAN / EXTENT
    rows = lax.broadcasted_iota(jnp.int32, (16, 128), 0) + (row_start - EXTENT // 2)
    cols = lax.broadcasted_iota(jnp.int32, (16, 128), 1) + (col_start - EXTENT // 2)
    rows = rows.astype(F32) * spacing
    cols = cols.astype(F32) * spacing
    elevation = jnp.sqrt(1.0 - rows * rows - cols * cols) - 1.0
    return screen_of(w * elevation)


def spread_block(load, block, twiddle, stacked):
    rows = pl.ds(pl.multiple_of(block * 16, 16), 16)
    for half in range(2):
        pairs = load(block, rows, half)
        re, im = dft8([pair[0] for pair in pairs], [pair[1] for pair in pairs])
        lanes = slice(128 * half, 128 * half + 128)
        other = slice(256 + 128 * half, 384 + 128 * half)
        for q in range(8):
            if q == 0:
                real, imag = re[0], im[0]
            else:
                cosine, sine = twiddle[0, q : q + 1, lanes], twiddle[1, q : q + 1, lanes]
                real, imag = re[q] * cosine - im[q] * sine, re[q] * sine + im[q] * cosine
            stacked[q, rows, lanes] = real.astype(BF16)
            stacked[q, rows, other] = imag.astype(BF16)


def turn_blocks(stacked, table, blocks):
    matrix = table[...]
    for pair in range(4):
        left = stacked[2 * pair : 2 * pair + 2].reshape(128, 512)
        out = jnp.dot(left, matrix, preferred_element_type=F32)
        for half in range(2):
            real, imag = slice(128 * half, 128 * half + 128), slice(256 + 128 * half, 384 + 128 * half)
            turned = []
            for item in range(2):
                rows = slice(64 * item, 64 * item + 64)
                square = jnp.concatenate([out[rows, real], out[rows, imag]], axis=0)
                turned.append(jnp.transpose(square).reshape(16, 8, 128))
            both = jnp.concatenate(turned, axis=1).astype(BF16)
            blocks[16 * half : 16 * half + 16, 16 * pair : 16 * pair + 16, :] = both


def gather_pair(pair, blocks, table, twiddle, middle):
    matrix = table[...]
    rows = blocks[:, pl.ds(pl.multiple_of(16 * pair, 16), 16), :].astype(F32)
    for item in range(2):
        q = 2 * pair + item
        flat = rows[:, 8 * item : 8 * item + 8, :].reshape(256, 128)
        low = jnp.transpose(flat[0:128]).astype(BF16)
        high = jnp.transpose(flat[128:256]).astype(BF16)
        left = jnp.concatenate([low[0:64], high[0:64], low[64:128], high[64:128]], axis=1)
        out = jnp.dot(left, matrix, preferred_element_type=F32)
        real, imag = out[:, 0:256], out[:, 256:512]
        cosine, sine = twiddle[0, pl.ds(q, 1), :], twiddle[1, pl.ds(q, 1), :]
        middle[q, :, 0:256] = real * cosine - imag * sine
        middle[q, :, 256:512] = real * sine + imag * cosine


def last_block(block, middle, emit):
    rows = pl.ds(pl.multiple_of(block * 16, 16), 16)
    for half in range(2):
        lanes = slice(128 * half, 128 * half + 128)
        other = slice(256 + 128 * half, 384 + 128 * half)
        re, im = dft8([middle[q, rows, lanes] for q in range(8)], [middle[q, rows, other] for q in range(8)])
        emit(block, rows, half, re, im)


def low_lanes():
    return lax.broadcasted_iota(jnp.int32, (16, 128), 1) < 64


def load_received(blocks):
    def load(block, rows, half):
        low = low_lanes()
        pairs = []
        for a in range(8):
            first = blocks[4 * a + 2 * half, rows, :].astype(F32)
            second = blocks[4 * a + 2 * half + 1, rows, :].astype(F32)
            pairs.append(
                (jnp.where(low, first, swap_halves(second)), jnp.where(low, swap_halves(first), second))
            )
        return pairs

    return load


def emit_blocks(blocks):
    def emit(block, rows, half, re, im):
        low = low_lanes()
        for a in range(8):
            blocks[4 * a + 2 * half, rows, :] = jnp.where(low, re[a], swap_halves(im[a])).astype(BF16)
            blocks[4 * a + 2 * half + 1, rows, :] = jnp.where(low, swap_halves(re[a]), im[a]).astype(BF16)

    return emit


def taps_of(position, places):
    distance = places - position
    inside = (distance > -4.0) & (distance <= 4.0)
    return jnp.where(inside, jnp.exp2(distance * distance * TAP_RATE), 0.0)


def place_index():
    place = lax.broadcasted_iota(jnp.int32, (TILE, V), 0)
    return (place // 8 + 8 * lax.rem(place, 8) - 3).astype(F32)


def grid_tile(tile, taps_u, taps_v, weight):
    partial = lax.dot_general(tile, taps_u, (((0,), (0,)), ((), ())), preferred_element_type=F32)
    real = jnp.sum(partial[0:64] * taps_v, axis=0, keepdims=True) * weight
    imag = jnp.sum(partial[64:128] * taps_v, axis=0, keepdims=True) * -weight
    spread = jnp.concatenate([taps_v * real, taps_v * imag], axis=0).astype(BF16)
    return lax.dot_general(taps_u, spread, (((1,), (1,)), ((), ())), preferred_element_type=F32).astype(BF16)


def chunk_rows(chunk):
    return pl.ds(pl.multiple_of(chunk * 16, 16), 16)


def send_all(axis, size, me, source, target, send, recv):
    def step(offset, carry):
        peer = lax.rem(me + offset, size)
        pltpu.make_async_remote_copy(
            source(peer), target, send, recv, device_id={axis: peer}, device_id_type=MESH
        ).start()
        return carry

    lax.fori_loop(1, size, step, 0)


def wait_recv(view, recv):
    pltpu.make_async_copy(view, view, recv).wait()


def greet(axis, size, me, barrier):
    def step(offset, carry):
        pl.semaphore_signal(
            barrier, inc=1, device_id={axis: lax.rem(me + offset, size)}, device_id_type=MESH
        )
        return carry

    lax.fori_loop(1, size, step, 0)


def whole_kernel(
    w_ref,
    owner,
    counts,
    image_in,
    positions_in,
    weights_in,
    table_in,
    twiddle_in,
    others,
    image,
    positions,
    weights,
    table,
    twiddle,
    packed,
    kept,
    got_packed,
    got_kept,
    stacked,
    blocks,
    got,
    tiles,
    gridded,
    back,
    got_back,
    middle,
    screen,
    terms,
    all_taps,
    tile_weight,
    local_sem,
    vis_send,
    vis_recv,
    out_send,
    out_recv,
    back_send,
    back_recv,
    term_send,
    term_recv,
):
    me = lax.axis_index("row")
    plane = lax.axis_index("plane")
    barrier = pltpu.get_barrier_semaphore()
    greet("row", ROWS, me, barrier)
    greet("plane", PLANES, plane, barrier)
    loads = [
        pltpu.make_async_copy(source, target, local_sem.at[index])
        for index, (source, target) in enumerate(
            (
                (image_in, image),
                (twiddle_in, twiddle),
                (positions_in, positions),
                (weights_in, weights),
                (table_in, table),
            )
        )
    ]
    for copy in loads:
        copy.start()
    w = w_ref[0]

    def load(block, rows, half):
        pairs = []
        for a in range(8):
            col = 256 * a + 128 * half
            cosine, sine = screen[0, rows, col : col + 128], screen[1, rows, col : col + 128]
            real, imag = image[0, rows, col : col + 128], image[1, rows, col : col + 128]
            pairs.append((real * cosine + imag * sine, real * sine - imag * cosine))
        return pairs

    def prepare(block, carry):
        rows = chunk_rows(block)
        for piece in range(16):
            lanes = slice(128 * piece, 128 * piece + 128)
            cosine, sine = chunk_screen(w, me * 64 + block * 16, 128 * piece)
            screen[0, rows, lanes] = cosine
            screen[1, rows, lanes] = sine
        return carry

    lax.fori_loop(0, 4, prepare, 0)
    for copy in loads[0:4]:
        copy.wait()
    place_of = lax.broadcasted_iota(jnp.int32, (1, V), 1)
    for peer in range(ROWS):
        pair = slice(2 * peer, 2 * peer + 2)
        packed[peer] = positions[0, 0, pair, :] * 8192 + positions[0, 1, pair, :]
        for item in range(2):
            slot = 2 * peer + item
            kept[peer, item : item + 1, :] = jnp.where(
                place_of < counts[0, slot], weights[0, slot : slot + 1, :], 0.0
            )

    def first_spread(block, carry):
        spread_block(load, block, twiddle, stacked)
        return carry

    lax.fori_loop(0, 4, first_spread, 0)
    loads[4].wait()
    turn_blocks(stacked, table, blocks)
    pl.semaphore_wait(barrier, ROWS + PLANES - 2)
    send_all("row", ROWS, me, lambda peer: packed.at[peer], got_packed.at[me], vis_send.at[0], vis_recv.at[0])
    send_all("row", ROWS, me, lambda peer: kept.at[peer], got_kept.at[me], vis_send.at[1], vis_recv.at[1])

    def send_chunk(chunk, carry):
        rows = chunk_rows(chunk)
        send_all(
            "row", ROWS, me, lambda peer: blocks.at[peer, rows], got.at[me, rows], out_send.at[chunk], out_recv.at[chunk]
        )
        return carry

    lax.fori_loop(0, 4, send_chunk, 0)
    got_packed[me] = packed[me]
    got_kept[me] = kept[me]
    got[me] = blocks[me]
    places = place_index()
    most = pl.ds(0, ROWS - 1)
    wait_recv(got_packed.at[most], vis_recv.at[0])
    wait_recv(got_kept.at[most], vis_recv.at[1])

    def tap_step(item, carry):
        name = owner[me * ROWS + item]

        def count(other, total):
            return total + jnp.where((owner[me * ROWS + other] == name) & (other < item), 1, 0)

        second = lax.fori_loop(0, ROWS, count, 0, unroll=True) > 0
        both, pair = got_packed[name], got_kept[name]
        place = jnp.where(second, both[1:2], both[0:1])
        u_part = place // 8192
        all_taps[item, 0] = taps_of(u_part.astype(F32) * (1.0 / OVER), places).astype(BF16)
        all_taps[item, 1] = taps_of((place - u_part * 8192).astype(F32) * (1.0 / OVER), places).astype(BF16)
        tile_weight[item] = jnp.where(second, pair[1:2], pair[0:1])
        return carry

    lax.fori_loop(0, ROWS, tap_step, 0)
    load_got = load_received(got)

    def second_spread(chunk, carry):
        wait_recv(got.at[most, chunk_rows(chunk)], out_recv.at[chunk])
        spread_block(load_got, chunk, twiddle, stacked)
        return carry

    lax.fori_loop(0, 4, second_spread, 0)
    turn_blocks(stacked, table, tiles)

    def grid_step(item, carry):
        gridded[item] = grid_tile(
            tiles[item], all_taps[item, 0], all_taps[item, 1].astype(F32), tile_weight[item]
        )
        return carry

    lax.fori_loop(0, ROWS, grid_step, 0, unroll=2)

    def gather_step(pair, carry):
        gather_pair(pair, gridded, table, twiddle, middle)
        return carry

    lax.fori_loop(0, 4, gather_step, 0)
    emit_back = emit_blocks(back)

    def back_chunk(chunk, carry):
        last_block(chunk, middle, emit_back)
        rows = chunk_rows(chunk)
        send_all(
            "row",
            ROWS,
            me,
            lambda peer: back.at[peer, rows],
            got_back.at[me, rows],
            back_send.at[chunk],
            back_recv.at[chunk],
        )
        return carry

    lax.fori_loop(0, 4, back_chunk, 0)
    got_back[me] = back[me]

    def final_gather(chunk, carry):
        wait_recv(got_back.at[most, chunk_rows(chunk)], back_recv.at[chunk])
        gather_pair(chunk, got_back, table, twiddle, middle)
        return carry

    lax.fori_loop(0, 4, final_gather, 0)

    def emit(block, rows, half, re, im):
        for a in range(8):
            lanes = slice(128 * half, 128 * half + 128)
            full = slice(256 * a + 128 * half, 256 * a + 128 * half + 128)
            cosine, sine = screen[0, rows, full], screen[1, rows, full]
            terms[a, 0, rows, lanes] = (re[a] * cosine - im[a] * sine).astype(BF16)
            terms[a, 1, rows, lanes] = (re[a] * sine + im[a] * cosine).astype(BF16)

    def term_chunk(chunk, carry):
        last_block(chunk, middle, emit)
        rows = chunk_rows(chunk)
        send_all(
            "plane", PLANES, plane, lambda peer: terms.at[peer, :, rows], others.at[plane, :, rows], term_send, term_recv
        )
        return carry

    lax.fori_loop(0, 4, term_chunk, 0)
    mine = pltpu.make_async_copy(terms.at[plane], others.at[plane], local_sem.at[0])
    mine.start()
    wait_recv(packed.at[most], vis_send.at[0])
    wait_recv(kept.at[most], vis_send.at[1])
    for chunk in range(4):
        wait_recv(blocks.at[most, chunk_rows(chunk)], out_send.at[chunk])
        wait_recv(back.at[most, chunk_rows(chunk)], back_send.at[chunk])
    mine.wait()
    rest = pl.ds(0, PLANES - 1)
    wait_recv(terms.at[rest], term_send)
    wait_recv(others.at[rest], term_recv)


def local(image, w_planes, owner, positions, weights, counts):
    table, twiddle = host_tables()
    smem = pl.BlockSpec(memory_space=pltpu.SMEM)
    anywhere = pl.BlockSpec(memory_space=pl.ANY)
    dma = pltpu.SemaphoreType.DMA
    block = pltpu.VMEM((ROWS, TILE, 128), BF16)
    others = pl.pallas_call(
        whole_kernel,
        out_shape=jax.ShapeDtypeStruct((PLANES, 2, 64, 256), BF16),
        in_specs=[smem] * 3 + [anywhere] * 5,
        out_specs=anywhere,
        scratch_shapes=[
            pltpu.VMEM((2, 64, EXTENT), F32),
            pltpu.VMEM((1, 2, 64, V), jnp.int32),
            pltpu.VMEM((1, 64, V), F32),
            pltpu.VMEM((512, 512), BF16),
            pltpu.VMEM((2, 8, 256), F32),
            pltpu.VMEM((ROWS, 2, V), jnp.int32),
            pltpu.VMEM((ROWS, 2, V), F32),
            pltpu.VMEM((ROWS, 2, V), jnp.int32),
            pltpu.VMEM((ROWS, 2, V), F32),
            pltpu.VMEM((8, 64, 512), BF16),
            block,
            block,
            block,
            block,
            block,
            block,
            pltpu.VMEM((8, 64, 512), F32),
            pltpu.VMEM((2, 64, EXTENT), F32),
            pltpu.VMEM((PLANES, 2, 64, 256), BF16),
            pltpu.VMEM((ROWS, 2, TILE, V), BF16),
            pltpu.VMEM((ROWS, 1, V), F32),
            dma((5,)),
            dma((2,)),
            dma((2,)),
            dma((4,)),
            dma((4,)),
            dma((4,)),
            dma((4,)),
            dma,
            dma,
        ],
        compiler_params=pltpu.CompilerParams(collective_id=0, has_side_effects=True),
        name="whole",
    )(
        w_planes,
        owner.reshape(-1),
        counts,
        image,
        positions,
        weights,
        jnp.asarray(table),
        jnp.asarray(twiddle),
    )
    return jnp.sum(others.astype(F32), axis=0)


def solution(mesh):
    in_specs = (
        P(None, "row", None),
        P("plane"),
        P("plane", None, None),
        P("plane", None, "row", None),
        P("plane", "row", None),
        P("plane", "row"),
    )
    out_specs = P(None, "row", "plane")
    return jax.shard_map(local, mesh=mesh, in_specs=in_specs, out_specs=out_specs, check_vma=False)
```

```python
import functools

import jax
import jax.numpy as jnp
import ml_dtypes
import numpy as np
from jax import lax
from jax.experimental import pallas as pl
from jax.experimental.pallas import tpu as pltpu
from jax.sharding import PartitionSpec as P

TILE = 64
S = 8
OVER = 128
V = 256
FIELD_SPAN = 0.7
EXTENT = 2048
ROWS = 32
PLANES = 8
SCALE = 1.0 / 2048.0
TAP_RATE = -4.0 * 1.4426950408889634
MESH = pl.DeviceIdType.MESH
F32 = jnp.float32
BF16 = jnp.bfloat16
ROOT = 0.7071067811865476
SIN_POLY = (6.283184916495429, -41.34158923268831, 81.59994332977428, -76.61447253115396, 41.342882354135696, -12.471243534350362)
COS_POLY = (0.9999999890590228, -19.739204499453827, 64.9391174598908, -85.45013953079768, 60.16763095026347, -25.967599245923736, 6.52865815775625)


def host_tables():
    index = np.arange(256)
    angle = 2.0 * np.pi / 256.0 * (index[:, None] * index[None, :] % 256)
    cosine, sine = np.cos(angle), np.sin(angle)
    table = np.block([[cosine, sine], [-sine, cosine]]).astype(ml_dtypes.bfloat16)
    turn = 2.0 * np.pi / 2048.0 * (np.arange(8)[:, None] * index[None, :])
    return table, np.stack([np.cos(turn), np.sin(turn)]).astype(np.float32)


def dft4(re, im):
    ar, ai, br, bi = re[0] + re[2], im[0] + im[2], re[0] - re[2], im[0] - im[2]
    cr, ci, dr, di = re[1] + re[3], im[1] + im[3], re[1] - re[3], im[1] - im[3]
    return [ar + cr, br - di, ar - cr, br + di], [ai + ci, bi + dr, ai - ci, bi - dr]


def dft8(re, im):
    er, ei = dft4(re[0::2], im[0::2])
    od, oi = dft4(re[1::2], im[1::2])
    tr = [od[0], (od[1] - oi[1]) * ROOT, -oi[2], (od[3] + oi[3]) * -ROOT]
    ti = [oi[0], (od[1] + oi[1]) * ROOT, od[2], (od[3] - oi[3]) * ROOT]
    return [er[k] + tr[k] for k in range(4)] + [er[k] - tr[k] for k in range(4)], [
        ei[k] + ti[k] for k in range(4)
    ] + [ei[k] - ti[k] for k in range(4)]


def swap_halves(value):
    return pltpu.roll(value, 64, 1)


def screen_of(turns):
    part = turns - jnp.round(turns)
    square = part * part
    sine = jnp.full_like(part, SIN_POLY[-1])
    for term in SIN_POLY[-2::-1]:
        sine = sine * square + term
    cosine = jnp.full_like(part, COS_POLY[-1])
    for term in COS_POLY[-2::-1]:
        cosine = cosine * square + term
    return cosine * SCALE, sine * part * SCALE


def chunk_screen(w, row_start, col_start):
    spacing = FIELD_SPAN / EXTENT
    rows = lax.broadcasted_iota(jnp.int32, (16, 128), 0) + (row_start - EXTENT // 2)
    cols = lax.broadcasted_iota(jnp.int32, (16, 128), 1) + (col_start - EXTENT // 2)
    rows = rows.astype(F32) * spacing
    cols = cols.astype(F32) * spacing
    elevation = jnp.sqrt(1.0 - rows * rows - cols * cols) - 1.0
    return screen_of(w * elevation)


def spread_block(load, block, twiddle, stacked):
    rows = pl.ds(pl.multiple_of(block * 16, 16), 16)
    for half in range(2):
        pairs = load(block, rows, half)
        re, im = dft8([pair[0] for pair in pairs], [pair[1] for pair in pairs])
        lanes = slice(128 * half, 128 * half + 128)
        other = slice(256 + 128 * half, 384 + 128 * half)
        for q in range(8):
            if q == 0:
                real, imag = re[0], im[0]
            else:
                cosine, sine = twiddle[0, q : q + 1, lanes], twiddle[1, q : q + 1, lanes]
                real, imag = re[q] * cosine - im[q] * sine, re[q] * sine + im[q] * cosine
            stacked[q, rows, lanes] = real.astype(BF16)
            stacked[q, rows, other] = imag.astype(BF16)


def turn_blocks(stacked, table, blocks):
    matrix = table[...]
    for pair in range(4):
        left = stacked[2 * pair : 2 * pair + 2].reshape(128, 512)
        out = jnp.dot(left, matrix, preferred_element_type=F32)
        for half in range(2):
            real, imag = slice(128 * half, 128 * half + 128), slice(256 + 128 * half, 384 + 128 * half)
            turned = []
            for item in range(2):
                rows = slice(64 * item, 64 * item + 64)
                square = jnp.concatenate([out[rows, real], out[rows, imag]], axis=0)
                turned.append(jnp.transpose(square).reshape(16, 8, 128))
            both = jnp.concatenate(turned, axis=1).astype(BF16)
            blocks[16 * half : 16 * half + 16, 16 * pair : 16 * pair + 16, :] = both


def gather_pair(pair, blocks, table, twiddle, middle):
    matrix = table[...]
    rows = blocks[:, pl.ds(pl.multiple_of(16 * pair, 16), 16), :].astype(F32)
    for item in range(2):
        q = 2 * pair + item
        flat = rows[:, 8 * item : 8 * item + 8, :].reshape(256, 128)
        low = jnp.transpose(flat[0:128]).astype(BF16)
        high = jnp.transpose(flat[128:256]).astype(BF16)
        left = jnp.concatenate([low[0:64], high[0:64], low[64:128], high[64:128]], axis=1)
        out = jnp.dot(left, matrix, preferred_element_type=F32)
        real, imag = out[:, 0:256], out[:, 256:512]
        cosine, sine = twiddle[0, pl.ds(q, 1), :], twiddle[1, pl.ds(q, 1), :]
        middle[q, :, 0:256] = real * cosine - imag * sine
        middle[q, :, 256:512] = real * sine + imag * cosine


def gather_chunk(chunk, blocks, table, twiddle, middle):
    values = blocks[chunk].astype(F32)
    left = []
    for item in range(2):
        flat = values[:, 8 * item : 8 * item + 8, :].reshape(256, 128)
        low = jnp.transpose(flat[0:128]).reshape(4, 2, 16, 128)
        high = jnp.transpose(flat[128:256]).reshape(4, 2, 16, 128)
        parts = [low[:, 0], high[:, 0], low[:, 1], high[:, 1]]
        left.append(jnp.concatenate([part.reshape(64, 128) for part in parts], axis=1))
    out = jnp.dot(jnp.concatenate(left, axis=0).astype(BF16), table[...], preferred_element_type=F32)
    rows = chunk_rows(chunk)
    for item in range(2):
        for place in range(4):
            q = 2 * place + item
            piece = out[64 * item + 16 * place : 64 * item + 16 * place + 16]
            real, imag = piece[:, 0:256], piece[:, 256:512]
            if q:
                cosine, sine = twiddle[0, q : q + 1, :], twiddle[1, q : q + 1, :]
                real, imag = real * cosine - imag * sine, real * sine + imag * cosine
            middle[q, rows, 0:256] = real
            middle[q, rows, 256:512] = imag


def last_block(block, middle, emit):
    rows = pl.ds(pl.multiple_of(block * 16, 16), 16)
    for half in range(2):
        lanes = slice(128 * half, 128 * half + 128)
        other = slice(256 + 128 * half, 384 + 128 * half)
        re, im = dft8([middle[q, rows, lanes] for q in range(8)], [middle[q, rows, other] for q in range(8)])
        emit(block, rows, half, re, im)


def low_lanes():
    return lax.broadcasted_iota(jnp.int32, (16, 128), 1) < 64


def load_received(blocks):
    def load(block, rows, half):
        low = low_lanes()
        pairs = []
        for a in range(8):
            first = blocks[4 * a + 2 * half, rows, :].astype(F32)
            second = blocks[4 * a + 2 * half + 1, rows, :].astype(F32)
            pairs.append(
                (jnp.where(low, first, swap_halves(second)), jnp.where(low, swap_halves(first), second))
            )
        return pairs

    return load


def emit_fields(fields):
    def emit(block, rows, half, re, im):
        for a in range(8):
            fields[2 * a + half, 0, rows, :] = re[a]
            fields[2 * a + half, 1, rows, :] = im[a]

    return emit


def shuffle_fields(fields, back):
    lane = lax.broadcasted_iota(jnp.int32, (16, 128), 1)
    for column in range(16):
        parts = [fields[column, index % 2, 16 * (index // 2) : 16 * (index // 2) + 16, :] for index in range(8)]
        for bit, shift in ((4, 64), (2, 32), (1, 16)):
            low = lax.rem(lane // shift, 2) == 0
            for index in range(8):
                if index & bit == 0:
                    first, second = parts[index], parts[index + bit]
                    parts[index] = jnp.where(low, first, pltpu.roll(second, shift, 1))
                    parts[index + bit] = jnp.where(low, pltpu.roll(first, 128 - shift, 1), second)
        for index in range(8):
            back[index % 4, 2 * column + index // 4] = parts[index].astype(BF16)


def taps_of(position, places):
    distance = places - position
    inside = (distance > -4.0) & (distance <= 4.0)
    return jnp.where(inside, jnp.exp2(distance * distance * TAP_RATE), 0.0)


def place_index():
    place = lax.broadcasted_iota(jnp.int32, (TILE, V), 0)
    return (place // 8 + 8 * lax.rem(place, 8) - 3).astype(F32)


def grid_tile(tile, taps_u, taps_v, weight):
    partial = lax.dot_general(tile, taps_u, (((0,), (0,)), ((), ())), preferred_element_type=F32)
    real = jnp.sum(partial[0:64] * taps_v, axis=0, keepdims=True) * weight
    imag = jnp.sum(partial[64:128] * taps_v, axis=0, keepdims=True) * -weight
    spread = jnp.concatenate([taps_v * real, taps_v * imag], axis=0).astype(BF16)
    return lax.dot_general(taps_u, spread, (((1,), (1,)), ((), ())), preferred_element_type=F32).astype(BF16)


def chunk_rows(chunk):
    return pl.ds(pl.multiple_of(chunk * 16, 16), 16)


def send_all(axis, size, me, source, target, send, recv):
    def step(offset, carry):
        peer = lax.rem(me + offset, size)
        pltpu.make_async_remote_copy(
            source(peer), target, send, recv, device_id={axis: peer}, device_id_type=MESH
        ).start()
        return carry

    lax.fori_loop(1, size, step, 0)


def wait_recv(view, recv):
    pltpu.make_async_copy(view, view, recv).wait()


def greet(axis, size, me, barrier):
    def step(offset, carry):
        pl.semaphore_signal(
            barrier, inc=1, device_id={axis: lax.rem(me + offset, size)}, device_id_type=MESH
        )
        return carry

    lax.fori_loop(1, size, step, 0)


def whole_kernel(
    w_ref,
    owner,
    counts,
    image_in,
    positions_in,
    weights_in,
    table_in,
    twiddle_in,
    others,
    image,
    positions,
    weights,
    table,
    twiddle,
    packed,
    kept,
    got_packed,
    got_kept,
    stacked,
    blocks,
    got,
    tiles,
    gridded,
    back,
    got_back,
    middle,
    screen,
    terms,
    all_taps,
    fields,
    names,
    seconds,
    local_sem,
    vis_send,
    vis_recv,
    out_send,
    out_recv,
    back_send,
    back_recv,
    term_send,
    term_recv,
):
    me = lax.axis_index("row")
    plane = lax.axis_index("plane")
    barrier = pltpu.get_barrier_semaphore()
    greet("row", ROWS, me, barrier)
    greet("plane", PLANES, plane, barrier)
    loads = [
        pltpu.make_async_copy(source, target, local_sem.at[index])
        for index, (source, target) in enumerate(
            (
                (image_in, image),
                (twiddle_in, twiddle),
                (positions_in, positions),
                (weights_in, weights),
                (table_in, table),
            )
        )
    ]
    for copy in loads:
        copy.start()
    w = w_ref[0]

    def load(block, rows, half):
        pairs = []
        for a in range(8):
            col = 256 * a + 128 * half
            cosine, sine = screen[0, rows, col : col + 128], screen[1, rows, col : col + 128]
            real, imag = image[0, rows, col : col + 128], image[1, rows, col : col + 128]
            pairs.append((real * cosine + imag * sine, real * sine - imag * cosine))
        return pairs

    def prepare(block, carry):
        rows = chunk_rows(block)
        for piece in range(16):
            lanes = slice(128 * piece, 128 * piece + 128)
            cosine, sine = chunk_screen(w, me * 64 + block * 16, 128 * piece)
            screen[0, rows, lanes] = cosine
            screen[1, rows, lanes] = sine
        return carry

    lax.fori_loop(0, 4, prepare, 0)
    for copy in loads[0:4]:
        copy.wait()
    place_of = lax.broadcasted_iota(jnp.int32, (1, V), 1)
    for peer in range(ROWS):
        pair = slice(2 * peer, 2 * peer + 2)
        packed[peer] = positions[0, 0, pair, :] * 8192 + positions[0, 1, pair, :]
        chosen = []
        for item in range(2):
            slot = 2 * peer + item
            chosen.append(jnp.where(place_of < counts[0, slot], weights[0, slot : slot + 1, :], 0.0))
        kept[peer] = jnp.concatenate(chosen, axis=0).astype(BF16)

    def first_spread(block, carry):
        spread_block(load, block, twiddle, stacked)
        return carry

    lax.fori_loop(0, 4, first_spread, 0)
    loads[4].wait()
    turn_blocks(stacked, table, blocks)
    pl.semaphore_wait(barrier, ROWS + PLANES - 2)
    send_all("row", ROWS, me, lambda peer: packed.at[peer], got_packed.at[me], vis_send.at[0], vis_recv.at[0])

    def send_chunk(chunk, carry):
        rows = chunk_rows(chunk)
        send_all(
            "row", ROWS, me, lambda peer: blocks.at[peer, rows], got.at[me, rows], out_send.at[chunk], out_recv.at[chunk]
        )
        return carry

    lax.fori_loop(0, 4, send_chunk, 0)
    send_all("row", ROWS, me, lambda peer: kept.at[peer], got_kept.at[me], vis_send.at[1], vis_recv.at[1])
    got_packed[me] = packed[me]
    got_kept[me] = kept[me]
    got[me] = blocks[me]
    places = place_index()
    most = pl.ds(0, ROWS - 1)
    wait_recv(got_packed.at[most], vis_recv.at[0])

    def tap_step(item, carry):
        name = owner[me * ROWS + item]

        def count(other, total):
            return total + jnp.where((owner[me * ROWS + other] == name) & (other < item), 1, 0)

        second = lax.fori_loop(0, ROWS, count, 0, unroll=True) > 0
        names[item] = name
        seconds[item] = jnp.where(second, 1, 0)
        both = got_packed[name]
        place = jnp.where(second, both[1:2], both[0:1])
        u_part = place // 8192
        all_taps[item, 0] = taps_of(u_part.astype(F32) * (1.0 / OVER), places).astype(BF16)
        all_taps[item, 1] = taps_of((place - u_part * 8192).astype(F32) * (1.0 / OVER), places).astype(BF16)
        return carry

    lax.fori_loop(0, ROWS, tap_step, 0)
    load_got = load_received(got)

    def second_spread(chunk, carry):
        wait_recv(got.at[most, chunk_rows(chunk)], out_recv.at[chunk])
        spread_block(load_got, chunk, twiddle, stacked)
        return carry

    lax.fori_loop(0, 4, second_spread, 0)
    turn_blocks(stacked, table, tiles)

    wait_recv(got_kept.at[most], vis_recv.at[1])
    for item in range(ROWS):
        pair = got_kept[names[item]].astype(F32)
        weight = jnp.where(seconds[item] > 0, pair[1:2], pair[0:1])
        gridded[item] = grid_tile(tiles[item], all_taps[item, 0], all_taps[item, 1].astype(F32), weight)
    for pair in range(4):
        gather_pair(pair, gridded, table, twiddle, middle)
    emit_back = emit_fields(fields)
    for block in range(4):
        last_block(block, middle, emit_back)
    shuffle_fields(fields, back)

    def back_chunk(chunk, carry):
        send_all(
            "row",
            ROWS,
            me,
            lambda peer: back.at[chunk, peer],
            got_back.at[chunk, me],
            back_send.at[chunk],
            back_recv.at[chunk],
        )
        got_back[chunk, me] = back[chunk, me]
        return carry

    lax.fori_loop(0, 4, back_chunk, 0)

    def emit(block, rows, half, re, im):
        for a in range(8):
            lanes = slice(128 * half, 128 * half + 128)
            full = slice(256 * a + 128 * half, 256 * a + 128 * half + 128)
            cosine, sine = screen[0, rows, full], screen[1, rows, full]
            terms[a, 0, rows, lanes] = (re[a] * cosine - im[a] * sine).astype(BF16)
            terms[a, 1, rows, lanes] = (re[a] * sine + im[a] * cosine).astype(BF16)

    def term_chunk(chunk, carry):
        wait_recv(got_back.at[chunk, most], back_recv.at[chunk])
        gather_chunk(chunk, got_back, table, twiddle, middle)
        last_block(chunk, middle, emit)
        rows = chunk_rows(chunk)
        send_all(
            "plane", PLANES, plane, lambda peer: terms.at[peer, :, rows], others.at[plane, :, rows], term_send, term_recv
        )
        return carry

    lax.fori_loop(0, 4, term_chunk, 0)
    mine = pltpu.make_async_copy(terms.at[plane], others.at[plane], local_sem.at[0])
    mine.start()
    wait_recv(packed.at[most], vis_send.at[0])
    wait_recv(kept.at[most], vis_send.at[1])
    for chunk in range(4):
        wait_recv(blocks.at[most, chunk_rows(chunk)], out_send.at[chunk])
        wait_recv(back.at[chunk, most], back_send.at[chunk])
    mine.wait()
    rest = pl.ds(0, PLANES - 1)
    wait_recv(terms.at[rest], term_send)
    wait_recv(others.at[rest], term_recv)


def local(image, w_planes, owner, positions, weights, counts):
    table, twiddle = host_tables()
    smem = pl.BlockSpec(memory_space=pltpu.SMEM)
    anywhere = pl.BlockSpec(memory_space=pl.ANY)
    dma = pltpu.SemaphoreType.DMA
    block = pltpu.VMEM((ROWS, TILE, 128), BF16)
    others = pl.pallas_call(
        whole_kernel,
        out_shape=jax.ShapeDtypeStruct((PLANES, 2, 64, 256), BF16),
        in_specs=[smem] * 3 + [anywhere] * 5,
        out_specs=anywhere,
        scratch_shapes=[
            pltpu.VMEM((2, 64, EXTENT), F32),
            pltpu.VMEM((1, 2, 64, V), jnp.int32),
            pltpu.VMEM((1, 64, V), F32),
            pltpu.VMEM((512, 512), BF16),
            pltpu.VMEM((2, 8, 256), F32),
            pltpu.VMEM((ROWS, 2, V), jnp.int32),
            pltpu.VMEM((ROWS, 2, V), BF16),
            pltpu.VMEM((ROWS, 2, V), jnp.int32),
            pltpu.VMEM((ROWS, 2, V), BF16),
            pltpu.VMEM((8, 64, 512), BF16),
            block,
            block,
            block,
            block,
            pltpu.VMEM((4, ROWS, 16, 128), BF16),
            pltpu.VMEM((4, ROWS, 16, 128), BF16),
            pltpu.VMEM((8, 64, 512), F32),
            pltpu.VMEM((2, 64, EXTENT), F32),
            pltpu.VMEM((PLANES, 2, 64, 256), BF16),
            pltpu.VMEM((ROWS, 2, TILE, V), BF16),
            pltpu.VMEM((16, 2, 64, 128), F32),
            pltpu.SMEM((ROWS,), jnp.int32),
            pltpu.SMEM((ROWS,), jnp.int32),
            dma((5,)),
            dma((2,)),
            dma((2,)),
            dma((4,)),
            dma((4,)),
            dma((4,)),
            dma((4,)),
            dma,
            dma,
        ],
        compiler_params=pltpu.CompilerParams(collective_id=0, has_side_effects=True),
        name="whole",
    )(
        w_planes,
        owner.reshape(-1),
        counts,
        image,
        positions,
        weights,
        jnp.asarray(table),
        jnp.asarray(twiddle),
    )
    return jnp.sum(others.astype(F32), axis=0)


def solution(mesh):
    in_specs = (
        P(None, "row", None),
        P("plane"),
        P("plane", None, None),
        P("plane", None, "row", None),
        P("plane", "row", None),
        P("plane", "row"),
    )
    out_specs = P(None, "row", "plane")
    return jax.shard_map(local, mesh=mesh, in_specs=in_specs, out_specs=out_specs, check_vma=False)
```

```python
import functools

import jax
import jax.numpy as jnp
import ml_dtypes
import numpy as np
from jax import lax
from jax.experimental import pallas as pl
from jax.experimental.pallas import tpu as pltpu
from jax.sharding import PartitionSpec as P

TILE = 64
S = 8
OVER = 128
V = 256
FIELD_SPAN = 0.7
EXTENT = 2048
ROWS = 32
PLANES = 8
SCALE = 1.0 / 2048.0
TAP_RATE = -4.0 * 1.4426950408889634
MESH = pl.DeviceIdType.MESH
F32 = jnp.float32
BF16 = jnp.bfloat16
ROOT = 0.7071067811865476
SIN_POLY = (6.283184916495429, -41.34158923268831, 81.59994332977428, -76.61447253115396, 41.342882354135696, -12.471243534350362)
COS_POLY = (0.9999999890590228, -19.739204499453827, 64.9391174598908, -85.45013953079768, 60.16763095026347, -25.967599245923736, 6.52865815775625)


def host_tables():
    index = np.arange(256)
    angle = 2.0 * np.pi / 256.0 * (index[:, None] * index[None, :] % 256)
    cosine, sine = np.cos(angle), np.sin(angle)
    table = np.block([[cosine, sine], [-sine, cosine]]).astype(ml_dtypes.bfloat16)
    turn = 2.0 * np.pi / 2048.0 * (np.arange(8)[:, None] * index[None, :])
    return table, np.stack([np.cos(turn), np.sin(turn)]).astype(np.float32)


def dft4(re, im):
    ar, ai, br, bi = re[0] + re[2], im[0] + im[2], re[0] - re[2], im[0] - im[2]
    cr, ci, dr, di = re[1] + re[3], im[1] + im[3], re[1] - re[3], im[1] - im[3]
    return [ar + cr, br - di, ar - cr, br + di], [ai + ci, bi + dr, ai - ci, bi - dr]


def dft8(re, im):
    er, ei = dft4(re[0::2], im[0::2])
    od, oi = dft4(re[1::2], im[1::2])
    tr = [od[0], (od[1] - oi[1]) * ROOT, -oi[2], (od[3] + oi[3]) * -ROOT]
    ti = [oi[0], (od[1] + oi[1]) * ROOT, od[2], (od[3] - oi[3]) * ROOT]
    return [er[k] + tr[k] for k in range(4)] + [er[k] - tr[k] for k in range(4)], [
        ei[k] + ti[k] for k in range(4)
    ] + [ei[k] - ti[k] for k in range(4)]


def swap_halves(value):
    return pltpu.roll(value, 64, 1)


def screen_of(turns):
    part = turns - jnp.round(turns)
    square = part * part
    sine = jnp.full_like(part, SIN_POLY[-1])
    for term in SIN_POLY[-2::-1]:
        sine = sine * square + term
    cosine = jnp.full_like(part, COS_POLY[-1])
    for term in COS_POLY[-2::-1]:
        cosine = cosine * square + term
    return cosine * SCALE, sine * part * SCALE


def chunk_screen(w, row_start, col_start):
    spacing = FIELD_SPAN / EXTENT
    rows = lax.broadcasted_iota(jnp.int32, (16, 128), 0) + (row_start - EXTENT // 2)
    cols = lax.broadcasted_iota(jnp.int32, (16, 128), 1) + (col_start - EXTENT // 2)
    rows = rows.astype(F32) * spacing
    cols = cols.astype(F32) * spacing
    elevation = jnp.sqrt(1.0 - rows * rows - cols * cols) - 1.0
    return screen_of(w * elevation)


def spread_block(load, block, twiddle, stacked):
    rows = pl.ds(pl.multiple_of(block * 16, 16), 16)
    for half in range(2):
        pairs = load(block, rows, half)
        re, im = dft8([pair[0] for pair in pairs], [pair[1] for pair in pairs])
        lanes = slice(128 * half, 128 * half + 128)
        other = slice(256 + 128 * half, 384 + 128 * half)
        for q in range(8):
            if q == 0:
                real, imag = re[0], im[0]
            else:
                cosine, sine = twiddle[0, q : q + 1, lanes], twiddle[1, q : q + 1, lanes]
                real, imag = re[q] * cosine - im[q] * sine, re[q] * sine + im[q] * cosine
            stacked[q, rows, lanes] = real.astype(BF16)
            stacked[q, rows, other] = imag.astype(BF16)


def turn_blocks(stacked, table, blocks):
    matrix = table[...]
    for pair in range(4):
        left = stacked[2 * pair : 2 * pair + 2].reshape(128, 512)
        out = jnp.dot(left, matrix, preferred_element_type=F32)
        for half in range(2):
            real, imag = slice(128 * half, 128 * half + 128), slice(256 + 128 * half, 384 + 128 * half)
            turned = []
            for item in range(2):
                rows = slice(64 * item, 64 * item + 64)
                square = jnp.concatenate([out[rows, real], out[rows, imag]], axis=0)
                turned.append(jnp.transpose(square).reshape(16, 8, 128))
            both = jnp.concatenate(turned, axis=1).astype(BF16)
            blocks[16 * half : 16 * half + 16, 16 * pair : 16 * pair + 16, :] = both


def gather_pair(pair, blocks, table, twiddle, middle):
    matrix = table[...]
    rows = blocks[:, pl.ds(pl.multiple_of(16 * pair, 16), 16), :].astype(F32)
    for item in range(2):
        q = 2 * pair + item
        flat = rows[:, 8 * item : 8 * item + 8, :].reshape(256, 128)
        low = jnp.transpose(flat[0:128]).astype(BF16)
        high = jnp.transpose(flat[128:256]).astype(BF16)
        left = jnp.concatenate([low[0:64], high[0:64], low[64:128], high[64:128]], axis=1)
        out = jnp.dot(left, matrix, preferred_element_type=F32)
        real, imag = out[:, 0:256], out[:, 256:512]
        cosine, sine = twiddle[0, pl.ds(q, 1), :], twiddle[1, pl.ds(q, 1), :]
        middle[q, :, 0:256] = real * cosine - imag * sine
        middle[q, :, 256:512] = real * sine + imag * cosine


def gather_chunk(chunk, blocks, table, twiddle, middle):
    values = blocks[chunk].astype(F32)
    left = []
    for item in range(2):
        flat = values[:, 8 * item : 8 * item + 8, :].reshape(256, 128)
        low = jnp.transpose(flat[0:128]).reshape(4, 2, 16, 128)
        high = jnp.transpose(flat[128:256]).reshape(4, 2, 16, 128)
        parts = [low[:, 0], high[:, 0], low[:, 1], high[:, 1]]
        left.append(jnp.concatenate([part.reshape(64, 128) for part in parts], axis=1))
    out = jnp.dot(jnp.concatenate(left, axis=0).astype(BF16), table[...], preferred_element_type=F32)
    rows = chunk_rows(chunk)
    for item in range(2):
        for place in range(4):
            q = 2 * place + item
            piece = out[64 * item + 16 * place : 64 * item + 16 * place + 16]
            real, imag = piece[:, 0:256], piece[:, 256:512]
            if q:
                cosine, sine = twiddle[0, q : q + 1, :], twiddle[1, q : q + 1, :]
                real, imag = real * cosine - imag * sine, real * sine + imag * cosine
            middle[q, rows, 0:256] = real
            middle[q, rows, 256:512] = imag


def last_block(block, middle, emit):
    rows = pl.ds(pl.multiple_of(block * 16, 16), 16)
    for half in range(2):
        lanes = slice(128 * half, 128 * half + 128)
        other = slice(256 + 128 * half, 384 + 128 * half)
        re, im = dft8([middle[q, rows, lanes] for q in range(8)], [middle[q, rows, other] for q in range(8)])
        emit(block, rows, half, re, im)


def low_lanes():
    return lax.broadcasted_iota(jnp.int32, (16, 128), 1) < 64


def load_received(blocks):
    def load(block, rows, half):
        low = low_lanes()
        pairs = []
        for a in range(8):
            first = blocks[4 * a + 2 * half, rows, :].astype(F32)
            second = blocks[4 * a + 2 * half + 1, rows, :].astype(F32)
            pairs.append(
                (jnp.where(low, first, swap_halves(second)), jnp.where(low, swap_halves(first), second))
            )
        return pairs

    return load


def emit_fields(fields):
    def emit(block, rows, half, re, im):
        for a in range(8):
            fields[2 * a + half, 0, rows, :] = re[a]
            fields[2 * a + half, 1, rows, :] = im[a]

    return emit


def shuffle_fields(fields, back):
    lane = lax.broadcasted_iota(jnp.int32, (16, 128), 1)
    for column in range(16):
        parts = [fields[column, index % 2, 16 * (index // 2) : 16 * (index // 2) + 16, :] for index in range(8)]
        for bit, shift in ((4, 64), (2, 32), (1, 16)):
            low = lax.rem(lane // shift, 2) == 0
            for index in range(8):
                if index & bit == 0:
                    first, second = parts[index], parts[index + bit]
                    parts[index] = jnp.where(low, first, pltpu.roll(second, shift, 1))
                    parts[index + bit] = jnp.where(low, pltpu.roll(first, 128 - shift, 1), second)
        for index in range(8):
            back[index % 4, 2 * column + index // 4] = parts[index].astype(BF16)


def taps_of(position, places):
    distance = places - position
    inside = (distance > -4.0) & (distance <= 4.0)
    return jnp.where(inside, jnp.exp2(distance * distance * TAP_RATE), 0.0)


def place_index():
    place = lax.broadcasted_iota(jnp.int32, (TILE, V), 0)
    return (place // 8 + 8 * lax.rem(place, 8) - 3).astype(F32)


def grid_tile(tile, taps_u, taps_v, weight):
    partial = lax.dot_general(tile, taps_u, (((0,), (0,)), ((), ())), preferred_element_type=F32)
    real = jnp.sum(partial[0:64] * taps_v, axis=0, keepdims=True) * weight
    imag = jnp.sum(partial[64:128] * taps_v, axis=0, keepdims=True) * -weight
    spread = jnp.concatenate([taps_v * real, taps_v * imag], axis=0).astype(BF16)
    return lax.dot_general(taps_u, spread, (((1,), (1,)), ((), ())), preferred_element_type=F32).astype(BF16)


def chunk_rows(chunk):
    return pl.ds(pl.multiple_of(chunk * 16, 16), 16)


def send_all(axis, size, me, source, target, send, recv):
    def step(offset, carry):
        peer = lax.rem(me + offset, size)
        pltpu.make_async_remote_copy(
            source(peer), target, send, recv, device_id={axis: peer}, device_id_type=MESH
        ).start()
        return carry

    lax.fori_loop(1, size, step, 0)


def wait_recv(view, recv):
    pltpu.make_async_copy(view, view, recv).wait()


def greet(axis, size, me, barrier):
    def step(offset, carry):
        pl.semaphore_signal(
            barrier, inc=1, device_id={axis: lax.rem(me + offset, size)}, device_id_type=MESH
        )
        return carry

    lax.fori_loop(1, size, step, 0)


def whole_kernel(
    w_ref,
    owner,
    counts,
    image_in,
    positions_in,
    weights_in,
    table_in,
    twiddle_in,
    others,
    image,
    positions,
    weights,
    table,
    twiddle,
    packed,
    kept,
    got_packed,
    got_kept,
    stacked,
    blocks,
    got,
    tiles,
    gridded,
    back,
    got_back,
    middle,
    screen,
    terms,
    all_taps,
    tile_weight,
    fields,
    names,
    seconds,
    local_sem,
    vis_send,
    vis_recv,
    out_send,
    out_recv,
    back_send,
    back_recv,
    term_send,
    term_recv,
):
    me = lax.axis_index("row")
    plane = lax.axis_index("plane")
    barrier = pltpu.get_barrier_semaphore()
    greet("row", ROWS, me, barrier)
    greet("plane", PLANES, plane, barrier)
    loads = [
        pltpu.make_async_copy(source, target, local_sem.at[index])
        for index, (source, target) in enumerate(
            (
                (image_in, image),
                (twiddle_in, twiddle),
                (positions_in, positions),
                (weights_in, weights),
                (table_in, table),
            )
        )
    ]
    for copy in loads:
        copy.start()
    w = w_ref[0]

    def load(block, rows, half):
        pairs = []
        for a in range(8):
            col = 256 * a + 128 * half
            cosine, sine = screen[0, rows, col : col + 128], screen[1, rows, col : col + 128]
            real, imag = image[0, rows, col : col + 128], image[1, rows, col : col + 128]
            pairs.append((real * cosine + imag * sine, real * sine - imag * cosine))
        return pairs

    def prepare(block, carry):
        rows = chunk_rows(block)
        for piece in range(16):
            lanes = slice(128 * piece, 128 * piece + 128)
            cosine, sine = chunk_screen(w, me * 64 + block * 16, 128 * piece)
            screen[0, rows, lanes] = cosine
            screen[1, rows, lanes] = sine
        return carry

    lax.fori_loop(0, 4, prepare, 0)
    for copy in loads[0:4]:
        copy.wait()
    place_of = lax.broadcasted_iota(jnp.int32, (1, V), 1)
    for peer in range(ROWS):
        pair = slice(2 * peer, 2 * peer + 2)
        packed[peer] = positions[0, 0, pair, :] * 8192 + positions[0, 1, pair, :]
        chosen = []
        for item in range(2):
            slot = 2 * peer + item
            chosen.append(jnp.where(place_of < counts[0, slot], weights[0, slot : slot + 1, :], 0.0))
        kept[peer] = jnp.concatenate(chosen, axis=0).astype(BF16)

    def first_spread(block, carry):
        spread_block(load, block, twiddle, stacked)
        return carry

    lax.fori_loop(0, 4, first_spread, 0)
    loads[4].wait()
    turn_blocks(stacked, table, blocks)
    pl.semaphore_wait(barrier, ROWS + PLANES - 2)
    send_all("row", ROWS, me, lambda peer: packed.at[peer], got_packed.at[me], vis_send.at[0], vis_recv.at[0])

    def send_chunk(chunk, carry):
        rows = chunk_rows(chunk)
        send_all(
            "row", ROWS, me, lambda peer: blocks.at[peer, rows], got.at[me, rows], out_send.at[chunk], out_recv.at[chunk]
        )
        return carry

    lax.fori_loop(0, 4, send_chunk, 0)
    send_all("row", ROWS, me, lambda peer: kept.at[peer], got_kept.at[me], vis_send.at[1], vis_recv.at[1])
    got_packed[me] = packed[me]
    got_kept[me] = kept[me]
    got[me] = blocks[me]
    places = place_index()
    most = pl.ds(0, ROWS - 1)
    wait_recv(got_packed.at[most], vis_recv.at[0])

    def tap_step(item, carry):
        name = owner[me * ROWS + item]

        def count(other, total):
            return total + jnp.where((owner[me * ROWS + other] == name) & (other < item), 1, 0)

        second = lax.fori_loop(0, ROWS, count, 0, unroll=True) > 0
        names[item] = name
        seconds[item] = jnp.where(second, 1, 0)
        both = got_packed[name]
        place = jnp.where(second, both[1:2], both[0:1])
        u_part = place // 8192
        all_taps[item, 0] = taps_of(u_part.astype(F32) * (1.0 / OVER), places).astype(BF16)
        all_taps[item, 1] = taps_of((place - u_part * 8192).astype(F32) * (1.0 / OVER), places).astype(BF16)
        return carry

    lax.fori_loop(0, ROWS, tap_step, 0)
    load_got = load_received(got)

    def second_spread(chunk, carry):
        wait_recv(got.at[most, chunk_rows(chunk)], out_recv.at[chunk])
        spread_block(load_got, chunk, twiddle, stacked)
        return carry

    lax.fori_loop(0, 4, second_spread, 0)
    turn_blocks(stacked, table, tiles)

    wait_recv(got_kept.at[most], vis_recv.at[1])
    for group in range(0, ROWS, 8):
        pairs = [got_kept[names[item]].astype(F32) for item in range(group, group + 8)]
        picked = [jnp.where(seconds[group + item] > 0, pairs[item][1:2], pairs[item][0:1]) for item in range(8)]
        for item in range(8):
            tile_weight[group + item] = picked[item]

    def grid_step(group, carry):
        for place in range(16):
            item = group * 16 + place
            gridded[item] = grid_tile(
                tiles[item], all_taps[item, 0], all_taps[item, 1].astype(F32), tile_weight[item]
            )
        return carry

    lax.fori_loop(0, 2, grid_step, 0)
    for pair in range(4):
        gather_pair(pair, gridded, table, twiddle, middle)
    emit_back = emit_fields(fields)
    for block in range(4):
        last_block(block, middle, emit_back)
    shuffle_fields(fields, back)

    def back_chunk(chunk, carry):
        send_all(
            "row",
            ROWS,
            me,
            lambda peer: back.at[chunk, peer],
            got_back.at[chunk, me],
            back_send.at[chunk],
            back_recv.at[chunk],
        )
        got_back[chunk, me] = back[chunk, me]
        return carry

    lax.fori_loop(0, 4, back_chunk, 0)

    def emit(block, rows, half, re, im):
        for a in range(8):
            lanes = slice(128 * half, 128 * half + 128)
            full = slice(256 * a + 128 * half, 256 * a + 128 * half + 128)
            cosine, sine = screen[0, rows, full], screen[1, rows, full]
            terms[a, 0, rows, lanes] = (re[a] * cosine - im[a] * sine).astype(BF16)
            terms[a, 1, rows, lanes] = (re[a] * sine + im[a] * cosine).astype(BF16)

    def term_chunk(chunk, carry):
        wait_recv(got_back.at[chunk, most], back_recv.at[chunk])
        gather_chunk(chunk, got_back, table, twiddle, middle)
        last_block(chunk, middle, emit)
        rows = chunk_rows(chunk)
        send_all(
            "plane", PLANES, plane, lambda peer: terms.at[peer, :, rows], others.at[plane, :, rows], term_send, term_recv
        )
        return carry

    lax.fori_loop(0, 4, term_chunk, 0)
    mine = pltpu.make_async_copy(terms.at[plane], others.at[plane], local_sem.at[0])
    mine.start()
    wait_recv(packed.at[most], vis_send.at[0])
    wait_recv(kept.at[most], vis_send.at[1])
    for chunk in range(4):
        wait_recv(blocks.at[most, chunk_rows(chunk)], out_send.at[chunk])
        wait_recv(back.at[chunk, most], back_send.at[chunk])
    mine.wait()
    rest = pl.ds(0, PLANES - 1)
    wait_recv(terms.at[rest], term_send)
    wait_recv(others.at[rest], term_recv)


def local(image, w_planes, owner, positions, weights, counts):
    table, twiddle = host_tables()
    smem = pl.BlockSpec(memory_space=pltpu.SMEM)
    anywhere = pl.BlockSpec(memory_space=pl.ANY)
    dma = pltpu.SemaphoreType.DMA
    block = pltpu.VMEM((ROWS, TILE, 128), BF16)
    others = pl.pallas_call(
        whole_kernel,
        out_shape=jax.ShapeDtypeStruct((PLANES, 2, 64, 256), BF16),
        in_specs=[smem] * 3 + [anywhere] * 5,
        out_specs=anywhere,
        scratch_shapes=[
            pltpu.VMEM((2, 64, EXTENT), F32),
            pltpu.VMEM((1, 2, 64, V), jnp.int32),
            pltpu.VMEM((1, 64, V), F32),
            pltpu.VMEM((512, 512), BF16),
            pltpu.VMEM((2, 8, 256), F32),
            pltpu.VMEM((ROWS, 2, V), jnp.int32),
            pltpu.VMEM((ROWS, 2, V), BF16),
            pltpu.VMEM((ROWS, 2, V), jnp.int32),
            pltpu.VMEM((ROWS, 2, V), BF16),
            pltpu.VMEM((8, 64, 512), BF16),
            block,
            block,
            block,
            block,
            pltpu.VMEM((4, ROWS, 16, 128), BF16),
            pltpu.VMEM((4, ROWS, 16, 128), BF16),
            pltpu.VMEM((8, 64, 512), F32),
            pltpu.VMEM((2, 64, EXTENT), F32),
            pltpu.VMEM((PLANES, 2, 64, 256), BF16),
            pltpu.VMEM((ROWS, 2, TILE, V), BF16),
            pltpu.VMEM((ROWS, 1, V), F32),
            pltpu.VMEM((16, 2, 64, 128), F32),
            pltpu.SMEM((ROWS,), jnp.int32),
            pltpu.SMEM((ROWS,), jnp.int32),
            dma((5,)),
            dma((2,)),
            dma((2,)),
            dma((4,)),
            dma((4,)),
            dma((4,)),
            dma((4,)),
            dma,
            dma,
        ],
        compiler_params=pltpu.CompilerParams(collective_id=0, has_side_effects=True),
        name="whole",
    )(
        w_planes,
        owner.reshape(-1),
        counts,
        image,
        positions,
        weights,
        jnp.asarray(table),
        jnp.asarray(twiddle),
    )
    return jnp.sum(others.astype(F32), axis=0)


def solution(mesh):
    in_specs = (
        P(None, "row", None),
        P("plane"),
        P("plane", None, None),
        P("plane", None, "row", None),
        P("plane", "row", None),
        P("plane", "row"),
    )
    out_specs = P(None, "row", "plane")
    return jax.shard_map(local, mesh=mesh, in_specs=in_specs, out_specs=out_specs, check_vma=False)
```

```python
import functools

import jax
import jax.numpy as jnp
import ml_dtypes
import numpy as np
from jax import lax
from jax.experimental import pallas as pl
from jax.experimental.pallas import tpu as pltpu
from jax.sharding import PartitionSpec as P

TILE = 64
S = 8
OVER = 128
V = 256
FIELD_SPAN = 0.7
EXTENT = 2048
ROWS = 32
PLANES = 8
SCALE = 1.0 / 2048.0
TAP_RATE = -4.0 * 1.4426950408889634
MESH = pl.DeviceIdType.MESH
F32 = jnp.float32
BF16 = jnp.bfloat16
ROOT = 0.7071067811865476
SIN_POLY = (6.283184916495429, -41.34158923268831, 81.59994332977428, -76.61447253115396, 41.342882354135696, -12.471243534350362)
COS_POLY = (0.9999999890590228, -19.739204499453827, 64.9391174598908, -85.45013953079768, 60.16763095026347, -25.967599245923736, 6.52865815775625)


def host_tables():
    index = np.arange(256)
    angle = 2.0 * np.pi / 256.0 * (index[:, None] * index[None, :] % 256)
    cosine, sine = np.cos(angle), np.sin(angle)
    table = np.block([[cosine, sine], [-sine, cosine]]).astype(ml_dtypes.bfloat16)
    turn = 2.0 * np.pi / 2048.0 * (np.arange(8)[:, None] * index[None, :])
    return table, np.stack([np.cos(turn), np.sin(turn)]).astype(np.float32)


def dft4(re, im):
    ar, ai, br, bi = re[0] + re[2], im[0] + im[2], re[0] - re[2], im[0] - im[2]
    cr, ci, dr, di = re[1] + re[3], im[1] + im[3], re[1] - re[3], im[1] - im[3]
    return [ar + cr, br - di, ar - cr, br + di], [ai + ci, bi + dr, ai - ci, bi - dr]


def dft8(re, im):
    er, ei = dft4(re[0::2], im[0::2])
    od, oi = dft4(re[1::2], im[1::2])
    tr = [od[0], (od[1] - oi[1]) * ROOT, -oi[2], (od[3] + oi[3]) * -ROOT]
    ti = [oi[0], (od[1] + oi[1]) * ROOT, od[2], (od[3] - oi[3]) * ROOT]
    return [er[k] + tr[k] for k in range(4)] + [er[k] - tr[k] for k in range(4)], [
        ei[k] + ti[k] for k in range(4)
    ] + [ei[k] - ti[k] for k in range(4)]


def swap_halves(value):
    return pltpu.roll(value, 64, 1)


def screen_of(turns):
    part = turns - jnp.round(turns)
    square = part * part
    sine = jnp.full_like(part, SIN_POLY[-1])
    for term in SIN_POLY[-2::-1]:
        sine = sine * square + term
    cosine = jnp.full_like(part, COS_POLY[-1])
    for term in COS_POLY[-2::-1]:
        cosine = cosine * square + term
    return cosine * SCALE, sine * part * SCALE


def chunk_screen(w, row_start, col_start):
    spacing = FIELD_SPAN / EXTENT
    rows = lax.broadcasted_iota(jnp.int32, (16, 128), 0) + (row_start - EXTENT // 2)
    cols = lax.broadcasted_iota(jnp.int32, (16, 128), 1) + (col_start - EXTENT // 2)
    rows = rows.astype(F32) * spacing
    cols = cols.astype(F32) * spacing
    elevation = jnp.sqrt(1.0 - rows * rows - cols * cols) - 1.0
    return screen_of(w * elevation)


def spread_block(load, block, twiddle, stacked):
    rows = pl.ds(pl.multiple_of(block * 16, 16), 16)
    for half in range(2):
        pairs = load(block, rows, half)
        re, im = dft8([pair[0] for pair in pairs], [pair[1] for pair in pairs])
        lanes = slice(128 * half, 128 * half + 128)
        other = slice(256 + 128 * half, 384 + 128 * half)
        for q in range(8):
            if q == 0:
                real, imag = re[0], im[0]
            else:
                cosine, sine = twiddle[0, q : q + 1, lanes], twiddle[1, q : q + 1, lanes]
                real, imag = re[q] * cosine - im[q] * sine, re[q] * sine + im[q] * cosine
            stacked[q, rows, lanes] = real.astype(BF16)
            stacked[q, rows, other] = imag.astype(BF16)


def turn_blocks(stacked, table, blocks):
    matrix = table[...]
    for pair in range(4):
        left = stacked[2 * pair : 2 * pair + 2].reshape(128, 512)
        out = jnp.dot(left, matrix, preferred_element_type=F32)
        for half in range(2):
            real, imag = slice(128 * half, 128 * half + 128), slice(256 + 128 * half, 384 + 128 * half)
            turned = []
            for item in range(2):
                rows = slice(64 * item, 64 * item + 64)
                square = jnp.concatenate([out[rows, real], out[rows, imag]], axis=0)
                turned.append(jnp.transpose(square).reshape(16, 8, 128))
            both = jnp.concatenate(turned, axis=1).astype(BF16)
            blocks[16 * half : 16 * half + 16, 16 * pair : 16 * pair + 16, :] = both


def gather_pair(pair, blocks, table, twiddle, middle):
    matrix = table[...]
    rows = blocks[:, pl.ds(pl.multiple_of(16 * pair, 16), 16), :].astype(F32)
    for item in range(2):
        q = 2 * pair + item
        flat = rows[:, 8 * item : 8 * item + 8, :].reshape(256, 128)
        low = jnp.transpose(flat[0:128]).astype(BF16)
        high = jnp.transpose(flat[128:256]).astype(BF16)
        left = jnp.concatenate([low[0:64], high[0:64], low[64:128], high[64:128]], axis=1)
        out = jnp.dot(left, matrix, preferred_element_type=F32)
        real, imag = out[:, 0:256], out[:, 256:512]
        cosine, sine = twiddle[0, pl.ds(q, 1), :], twiddle[1, pl.ds(q, 1), :]
        middle[q, :, 0:256] = real * cosine - imag * sine
        middle[q, :, 256:512] = real * sine + imag * cosine


def gather_chunk(chunk, blocks, table, twiddle, middle):
    values = blocks[chunk].astype(F32)
    left = []
    for item in range(2):
        flat = values[:, 8 * item : 8 * item + 8, :].reshape(256, 128)
        low = jnp.transpose(flat[0:128]).reshape(4, 2, 16, 128)
        high = jnp.transpose(flat[128:256]).reshape(4, 2, 16, 128)
        parts = [low[:, 0], high[:, 0], low[:, 1], high[:, 1]]
        left.append(jnp.concatenate([part.reshape(64, 128) for part in parts], axis=1))
    out = jnp.dot(jnp.concatenate(left, axis=0).astype(BF16), table[...], preferred_element_type=F32)
    rows = chunk_rows(chunk)
    for item in range(2):
        for place in range(4):
            q = 2 * place + item
            piece = out[64 * item + 16 * place : 64 * item + 16 * place + 16]
            real, imag = piece[:, 0:256], piece[:, 256:512]
            if q:
                cosine, sine = twiddle[0, q : q + 1, :], twiddle[1, q : q + 1, :]
                real, imag = real * cosine - imag * sine, real * sine + imag * cosine
            middle[q, rows, 0:256] = real
            middle[q, rows, 256:512] = imag


def last_block(block, middle, emit):
    rows = pl.ds(pl.multiple_of(block * 16, 16), 16)
    for half in range(2):
        lanes = slice(128 * half, 128 * half + 128)
        other = slice(256 + 128 * half, 384 + 128 * half)
        re, im = dft8([middle[q, rows, lanes] for q in range(8)], [middle[q, rows, other] for q in range(8)])
        emit(block, rows, half, re, im)


def low_lanes():
    return lax.broadcasted_iota(jnp.int32, (16, 128), 1) < 64


def load_received(blocks):
    def load(block, rows, half):
        low = low_lanes()
        pairs = []
        for a in range(8):
            first = blocks[4 * a + 2 * half, rows, :].astype(F32)
            second = blocks[4 * a + 2 * half + 1, rows, :].astype(F32)
            pairs.append(
                (jnp.where(low, first, swap_halves(second)), jnp.where(low, swap_halves(first), second))
            )
        return pairs

    return load


def emit_fields(fields):
    def emit(block, rows, half, re, im):
        for a in range(8):
            fields[2 * a + half, 0, rows, :] = re[a]
            fields[2 * a + half, 1, rows, :] = im[a]

    return emit


def shuffle_fields(fields, back):
    lane = lax.broadcasted_iota(jnp.int32, (16, 128), 1)
    for column in range(16):
        parts = [fields[column, index % 2, 16 * (index // 2) : 16 * (index // 2) + 16, :] for index in range(8)]
        for bit, shift in ((4, 64), (2, 32), (1, 16)):
            low = lax.rem(lane // shift, 2) == 0
            for index in range(8):
                if index & bit == 0:
                    first, second = parts[index], parts[index + bit]
                    parts[index] = jnp.where(low, first, pltpu.roll(second, shift, 1))
                    parts[index + bit] = jnp.where(low, pltpu.roll(first, 128 - shift, 1), second)
        for index in range(8):
            back[index % 4, 2 * column + index // 4] = parts[index].astype(BF16)


def taps_of(position, places):
    distance = places - position
    inside = (distance > -4.0) & (distance <= 4.0)
    return jnp.where(inside, jnp.exp2(distance * distance * TAP_RATE), 0.0)


def place_index():
    place = lax.broadcasted_iota(jnp.int32, (TILE, V), 0)
    return (place // 8 + 8 * lax.rem(place, 8) - 3).astype(F32)


def grid_tile(tile, taps_u, taps_v, weight):
    partial = lax.dot_general(tile, taps_u, (((0,), (0,)), ((), ())), preferred_element_type=F32)
    real = jnp.sum(partial[0:64] * taps_v, axis=0, keepdims=True) * weight
    imag = jnp.sum(partial[64:128] * taps_v, axis=0, keepdims=True) * -weight
    spread = jnp.concatenate([taps_v * real, taps_v * imag], axis=0).astype(BF16)
    return lax.dot_general(taps_u, spread, (((1,), (1,)), ((), ())), preferred_element_type=F32).astype(BF16)


def chunk_rows(chunk):
    return pl.ds(pl.multiple_of(chunk * 16, 16), 16)


def send_all(axis, size, me, source, target, send, recv):
    def step(offset, carry):
        peer = lax.rem(me + offset, size)
        pltpu.make_async_remote_copy(
            source(peer), target, send, recv, device_id={axis: peer}, device_id_type=MESH
        ).start()
        return carry

    lax.fori_loop(1, size, step, 0)


def wait_recv(view, recv):
    pltpu.make_async_copy(view, view, recv).wait()


def greet(axis, size, me, barrier):
    def step(offset, carry):
        pl.semaphore_signal(
            barrier, inc=1, device_id={axis: lax.rem(me + offset, size)}, device_id_type=MESH
        )
        return carry

    lax.fori_loop(1, size, step, 0)


def whole_kernel(
    w_ref,
    owner_in,
    counts_in,
    image_in,
    positions_in,
    weights_in,
    table_in,
    twiddle_in,
    others,
    owner,
    counts,
    image,
    positions,
    weights,
    table,
    twiddle,
    packed,
    kept,
    got_packed,
    got_kept,
    stacked,
    blocks,
    got,
    tiles,
    gridded,
    back,
    got_back,
    middle,
    screen,
    terms,
    all_taps,
    tile_weight,
    fields,
    names,
    seconds,
    local_sem,
    vis_send,
    vis_recv,
    out_send,
    out_recv,
    back_send,
    back_recv,
    term_send,
    term_recv,
):
    me = lax.axis_index("row")
    plane = lax.axis_index("plane")
    barrier = pltpu.get_barrier_semaphore()
    greet("row", ROWS, me, barrier)
    greet("plane", PLANES, plane, barrier)
    loads = [
        pltpu.make_async_copy(source, target, local_sem.at[index])
        for index, (source, target) in enumerate(
            (
                (owner_in, owner),
                (counts_in, counts),
                (image_in, image),
                (twiddle_in, twiddle),
                (positions_in, positions),
                (weights_in, weights),
                (table_in, table),
            )
        )
    ]
    for copy in loads:
        copy.start()
    w = w_ref[0]

    def load(block, rows, half):
        pairs = []
        for a in range(8):
            col = 256 * a + 128 * half
            cosine, sine = screen[0, rows, col : col + 128], screen[1, rows, col : col + 128]
            real, imag = image[0, rows, col : col + 128], image[1, rows, col : col + 128]
            pairs.append((real * cosine + imag * sine, real * sine - imag * cosine))
        return pairs

    def prepare(block, carry):
        rows = chunk_rows(block)
        for piece in range(16):
            lanes = slice(128 * piece, 128 * piece + 128)
            cosine, sine = chunk_screen(w, me * 64 + block * 16, 128 * piece)
            screen[0, rows, lanes] = cosine
            screen[1, rows, lanes] = sine
        return carry

    lax.fori_loop(0, 4, prepare, 0)
    for copy in loads[0:6]:
        copy.wait()
    place_of = lax.broadcasted_iota(jnp.int32, (1, V), 1)
    for peer in range(ROWS):
        pair = slice(2 * peer, 2 * peer + 2)
        packed[peer] = positions[0, 0, pair, :] * 8192 + positions[0, 1, pair, :]
        chosen = []
        for item in range(2):
            slot = 2 * peer + item
            chosen.append(jnp.where(place_of < counts[0, slot], weights[0, slot : slot + 1, :], 0.0))
        kept[peer] = jnp.concatenate(chosen, axis=0).astype(BF16)

    def first_spread(block, carry):
        spread_block(load, block, twiddle, stacked)
        return carry

    lax.fori_loop(0, 4, first_spread, 0)
    pl.semaphore_wait(barrier, ROWS + PLANES - 2)
    send_all("row", ROWS, me, lambda peer: packed.at[peer], got_packed.at[me], vis_send.at[0], vis_recv.at[0])
    loads[6].wait()
    turn_blocks(stacked, table, blocks)

    def send_chunk(chunk, carry):
        rows = chunk_rows(chunk)
        send_all(
            "row", ROWS, me, lambda peer: blocks.at[peer, rows], got.at[me, rows], out_send.at[chunk], out_recv.at[chunk]
        )
        return carry

    lax.fori_loop(0, 4, send_chunk, 0)
    send_all("row", ROWS, me, lambda peer: kept.at[peer], got_kept.at[me], vis_send.at[1], vis_recv.at[1])
    got_packed[me] = packed[me]
    got_kept[me] = kept[me]
    got[me] = blocks[me]
    places = place_index()
    most = pl.ds(0, ROWS - 1)
    wait_recv(got_packed.at[most], vis_recv.at[0])

    def tap_step(item, carry):
        name = owner[me * ROWS + item]

        def count(other, total):
            return total + jnp.where((owner[me * ROWS + other] == name) & (other < item), 1, 0)

        second = lax.fori_loop(0, ROWS, count, 0, unroll=True) > 0
        names[item] = name
        seconds[item] = jnp.where(second, 1, 0)
        both = got_packed[name]
        place = jnp.where(second, both[1:2], both[0:1])
        u_part = place // 8192
        all_taps[item, 0] = taps_of(u_part.astype(F32) * (1.0 / OVER), places).astype(BF16)
        all_taps[item, 1] = taps_of((place - u_part * 8192).astype(F32) * (1.0 / OVER), places).astype(BF16)
        return carry

    lax.fori_loop(0, ROWS, tap_step, 0)
    load_got = load_received(got)

    def second_spread(chunk, carry):
        wait_recv(got.at[most, chunk_rows(chunk)], out_recv.at[chunk])
        spread_block(load_got, chunk, twiddle, stacked)
        return carry

    lax.fori_loop(0, 4, second_spread, 0)
    turn_blocks(stacked, table, tiles)

    wait_recv(got_kept.at[most], vis_recv.at[1])
    for group in range(0, ROWS, 8):
        pairs = [got_kept[names[item]].astype(F32) for item in range(group, group + 8)]
        picked = [jnp.where(seconds[group + item] > 0, pairs[item][1:2], pairs[item][0:1]) for item in range(8)]
        for item in range(8):
            tile_weight[group + item] = picked[item]

    def grid_step(group, carry):
        for place in range(16):
            item = group * 16 + place
            gridded[item] = grid_tile(
                tiles[item], all_taps[item, 0], all_taps[item, 1].astype(F32), tile_weight[item]
            )
        return carry

    lax.fori_loop(0, 2, grid_step, 0)
    for pair in range(4):
        gather_pair(pair, gridded, table, twiddle, middle)
    emit_back = emit_fields(fields)
    for block in range(4):
        last_block(block, middle, emit_back)
    shuffle_fields(fields, back)

    def back_chunk(chunk, carry):
        send_all(
            "row",
            ROWS,
            me,
            lambda peer: back.at[chunk, peer],
            got_back.at[chunk, me],
            back_send.at[chunk],
            back_recv.at[chunk],
        )
        got_back[chunk, me] = back[chunk, me]
        return carry

    lax.fori_loop(0, 4, back_chunk, 0)

    def emit(block, rows, half, re, im):
        for a in range(8):
            lanes = slice(128 * half, 128 * half + 128)
            full = slice(256 * a + 128 * half, 256 * a + 128 * half + 128)
            cosine, sine = screen[0, rows, full], screen[1, rows, full]
            terms[a, 0, rows, lanes] = (re[a] * cosine - im[a] * sine).astype(BF16)
            terms[a, 1, rows, lanes] = (re[a] * sine + im[a] * cosine).astype(BF16)

    def term_chunk(chunk, carry):
        wait_recv(got_back.at[chunk, most], back_recv.at[chunk])
        gather_chunk(chunk, got_back, table, twiddle, middle)
        last_block(chunk, middle, emit)
        rows = chunk_rows(chunk)
        send_all(
            "plane", PLANES, plane, lambda peer: terms.at[peer, :, rows], others.at[plane, :, rows], term_send, term_recv
        )
        return carry

    lax.fori_loop(0, 4, term_chunk, 0)
    mine = pltpu.make_async_copy(terms.at[plane], others.at[plane], local_sem.at[0])
    mine.start()
    wait_recv(packed.at[most], vis_send.at[0])
    wait_recv(kept.at[most], vis_send.at[1])
    for chunk in range(4):
        wait_recv(blocks.at[most, chunk_rows(chunk)], out_send.at[chunk])
        wait_recv(back.at[chunk, most], back_send.at[chunk])
    mine.wait()
    rest = pl.ds(0, PLANES - 1)
    wait_recv(terms.at[rest], term_send)
    wait_recv(others.at[rest], term_recv)


def local(image, w_planes, owner, positions, weights, counts):
    table, twiddle = host_tables()
    smem = pl.BlockSpec(memory_space=pltpu.SMEM)
    anywhere = pl.BlockSpec(memory_space=pl.ANY)
    dma = pltpu.SemaphoreType.DMA
    block = pltpu.VMEM((ROWS, TILE, 128), BF16)
    others = pl.pallas_call(
        whole_kernel,
        out_shape=jax.ShapeDtypeStruct((PLANES, 2, 64, 256), BF16),
        in_specs=[smem] + [pl.BlockSpec(memory_space=pltpu.HBM)] * 7,
        out_specs=anywhere,
        scratch_shapes=[
            pltpu.SMEM((ROWS * ROWS,), jnp.int32),
            pltpu.SMEM((1, 64), jnp.int32),
            pltpu.VMEM((2, 64, EXTENT), F32),
            pltpu.VMEM((1, 2, 64, V), jnp.int32),
            pltpu.VMEM((1, 64, V), F32),
            pltpu.VMEM((512, 512), BF16),
            pltpu.VMEM((2, 8, 256), F32),
            pltpu.VMEM((ROWS, 2, V), jnp.int32),
            pltpu.VMEM((ROWS, 2, V), BF16),
            pltpu.VMEM((ROWS, 2, V), jnp.int32),
            pltpu.VMEM((ROWS, 2, V), BF16),
            pltpu.VMEM((8, 64, 512), BF16),
            block,
            block,
            block,
            block,
            pltpu.VMEM((4, ROWS, 16, 128), BF16),
            pltpu.VMEM((4, ROWS, 16, 128), BF16),
            pltpu.VMEM((8, 64, 512), F32),
            pltpu.VMEM((2, 64, EXTENT), F32),
            pltpu.VMEM((PLANES, 2, 64, 256), BF16),
            pltpu.VMEM((ROWS, 2, TILE, V), BF16),
            pltpu.VMEM((ROWS, 1, V), F32),
            pltpu.VMEM((16, 2, 64, 128), F32),
            pltpu.SMEM((ROWS,), jnp.int32),
            pltpu.SMEM((ROWS,), jnp.int32),
            dma((7,)),
            dma((2,)),
            dma((2,)),
            dma((4,)),
            dma((4,)),
            dma((4,)),
            dma((4,)),
            dma,
            dma,
        ],
        compiler_params=pltpu.CompilerParams(collective_id=0, has_side_effects=True, vmem_limit_bytes=24 * 1024 * 1024),
        name="whole",
    )(
        w_planes,
        *[
            pltpu.with_memory_space_constraint(value, pltpu.HBM)
            for value in (
                owner.reshape(-1),
                counts,
                image,
                positions,
                weights,
                jnp.asarray(table),
                jnp.asarray(twiddle),
            )
        ],
    )
    return jnp.sum(others.astype(F32), axis=0)


def solution(mesh):
    in_specs = (
        P(None, "row", None),
        P("plane"),
        P("plane", None, None),
        P("plane", None, "row", None),
        P("plane", "row", None),
        P("plane", "row"),
    )
    out_specs = P(None, "row", "plane")
    return jax.shard_map(local, mesh=mesh, in_specs=in_specs, out_specs=out_specs, check_vma=False)
```

```python
import functools

import jax
import jax.numpy as jnp
import ml_dtypes
import numpy as np
from jax import lax
from jax.experimental import pallas as pl
from jax.experimental.pallas import tpu as pltpu
from jax.sharding import PartitionSpec as P

TILE = 64
S = 8
OVER = 128
V = 256
FIELD_SPAN = 0.7
EXTENT = 2048
ROWS = 32
PLANES = 8
SCALE = 1.0 / 2048.0
TAP_RATE = -4.0 * 1.4426950408889634
MESH = pl.DeviceIdType.MESH
F32 = jnp.float32
BF16 = jnp.bfloat16
ROOT = 0.7071067811865476
SIN_POLY = (6.283184916495429, -41.34158923268831, 81.59994332977428, -76.61447253115396, 41.342882354135696, -12.471243534350362)
COS_POLY = (0.9999999890590228, -19.739204499453827, 64.9391174598908, -85.45013953079768, 60.16763095026347, -25.967599245923736, 6.52865815775625)


def host_tables():
    index = np.arange(256)
    angle = 2.0 * np.pi / 256.0 * (index[:, None] * index[None, :] % 256)
    cosine, sine = np.cos(angle), np.sin(angle)
    table = np.block([[cosine, sine], [-sine, cosine]]).astype(ml_dtypes.bfloat16)
    turn = 2.0 * np.pi / 2048.0 * (np.arange(8)[:, None] * index[None, :])
    return table, np.stack([np.cos(turn), np.sin(turn)]).astype(np.float32)


def dft4(re, im):
    ar, ai, br, bi = re[0] + re[2], im[0] + im[2], re[0] - re[2], im[0] - im[2]
    cr, ci, dr, di = re[1] + re[3], im[1] + im[3], re[1] - re[3], im[1] - im[3]
    return [ar + cr, br - di, ar - cr, br + di], [ai + ci, bi + dr, ai - ci, bi - dr]


def dft8(re, im):
    er, ei = dft4(re[0::2], im[0::2])
    od, oi = dft4(re[1::2], im[1::2])
    tr = [od[0], (od[1] - oi[1]) * ROOT, -oi[2], (od[3] + oi[3]) * -ROOT]
    ti = [oi[0], (od[1] + oi[1]) * ROOT, od[2], (od[3] - oi[3]) * ROOT]
    return [er[k] + tr[k] for k in range(4)] + [er[k] - tr[k] for k in range(4)], [
        ei[k] + ti[k] for k in range(4)
    ] + [ei[k] - ti[k] for k in range(4)]


def swap_halves(value):
    return pltpu.roll(value, 64, 1)


def screen_of(turns):
    part = turns - jnp.round(turns)
    square = part * part
    sine = jnp.full_like(part, SIN_POLY[-1])
    for term in SIN_POLY[-2::-1]:
        sine = sine * square + term
    cosine = jnp.full_like(part, COS_POLY[-1])
    for term in COS_POLY[-2::-1]:
        cosine = cosine * square + term
    return cosine * SCALE, sine * part * SCALE


def chunk_screen(w, row_start, col_start):
    spacing = FIELD_SPAN / EXTENT
    rows = lax.broadcasted_iota(jnp.int32, (16, 128), 0) + (row_start - EXTENT // 2)
    cols = lax.broadcasted_iota(jnp.int32, (16, 128), 1) + (col_start - EXTENT // 2)
    rows = rows.astype(F32) * spacing
    cols = cols.astype(F32) * spacing
    elevation = jnp.sqrt(1.0 - rows * rows - cols * cols) - 1.0
    return screen_of(w * elevation)


def spread_block(load, block, twiddle, stacked):
    rows = pl.ds(pl.multiple_of(block * 16, 16), 16)
    for half in range(2):
        pairs = load(block, rows, half)
        re, im = dft8([pair[0] for pair in pairs], [pair[1] for pair in pairs])
        lanes = slice(128 * half, 128 * half + 128)
        other = slice(256 + 128 * half, 384 + 128 * half)
        for q in range(8):
            if q == 0:
                real, imag = re[0], im[0]
            else:
                cosine, sine = twiddle[0, q : q + 1, lanes], twiddle[1, q : q + 1, lanes]
                real, imag = re[q] * cosine - im[q] * sine, re[q] * sine + im[q] * cosine
            stacked[q, rows, lanes] = real.astype(BF16)
            stacked[q, rows, other] = imag.astype(BF16)


def turn_blocks(stacked, table, blocks):
    matrix = table[...]
    for pair in range(4):
        left = stacked[2 * pair : 2 * pair + 2].reshape(128, 512)
        out = jnp.dot(left, matrix, preferred_element_type=F32)
        for half in range(2):
            real, imag = slice(128 * half, 128 * half + 128), slice(256 + 128 * half, 384 + 128 * half)
            turned = []
            for item in range(2):
                rows = slice(64 * item, 64 * item + 64)
                square = jnp.concatenate([out[rows, real], out[rows, imag]], axis=0)
                turned.append(jnp.transpose(square).reshape(16, 8, 128))
            both = jnp.concatenate(turned, axis=1).astype(BF16)
            blocks[16 * half : 16 * half + 16, 16 * pair : 16 * pair + 16, :] = both


def gather_pair(pair, blocks, table, twiddle, middle):
    matrix = table[...]
    rows = blocks[:, pl.ds(pl.multiple_of(16 * pair, 16), 16), :].astype(F32)
    for item in range(2):
        q = 2 * pair + item
        flat = rows[:, 8 * item : 8 * item + 8, :].reshape(256, 128)
        low = jnp.transpose(flat[0:128]).astype(BF16)
        high = jnp.transpose(flat[128:256]).astype(BF16)
        left = jnp.concatenate([low[0:64], high[0:64], low[64:128], high[64:128]], axis=1)
        out = jnp.dot(left, matrix, preferred_element_type=F32)
        real, imag = out[:, 0:256], out[:, 256:512]
        cosine, sine = twiddle[0, pl.ds(q, 1), :], twiddle[1, pl.ds(q, 1), :]
        middle[q, :, 0:256] = real * cosine - imag * sine
        middle[q, :, 256:512] = real * sine + imag * cosine


def gather_chunk(chunk, blocks, table, twiddle, middle):
    values = blocks[chunk].astype(F32)
    left = []
    for item in range(2):
        flat = values[:, 8 * item : 8 * item + 8, :].reshape(256, 128)
        low = jnp.transpose(flat[0:128]).reshape(4, 2, 16, 128)
        high = jnp.transpose(flat[128:256]).reshape(4, 2, 16, 128)
        parts = [low[:, 0], high[:, 0], low[:, 1], high[:, 1]]
        left.append(jnp.concatenate([part.reshape(64, 128) for part in parts], axis=1))
    out = jnp.dot(jnp.concatenate(left, axis=0).astype(BF16), table[...], preferred_element_type=F32)
    rows = chunk_rows(chunk)
    for item in range(2):
        for place in range(4):
            q = 2 * place + item
            piece = out[64 * item + 16 * place : 64 * item + 16 * place + 16]
            real, imag = piece[:, 0:256], piece[:, 256:512]
            if q:
                cosine, sine = twiddle[0, q : q + 1, :], twiddle[1, q : q + 1, :]
                real, imag = real * cosine - imag * sine, real * sine + imag * cosine
            middle[q, rows, 0:256] = real
            middle[q, rows, 256:512] = imag


def last_block(block, middle, emit):
    rows = pl.ds(pl.multiple_of(block * 16, 16), 16)
    for half in range(2):
        lanes = slice(128 * half, 128 * half + 128)
        other = slice(256 + 128 * half, 384 + 128 * half)
        re, im = dft8([middle[q, rows, lanes] for q in range(8)], [middle[q, rows, other] for q in range(8)])
        emit(block, rows, half, re, im)


def low_lanes():
    return lax.broadcasted_iota(jnp.int32, (16, 128), 1) < 64


def load_received(blocks):
    def load(block, rows, half):
        low = low_lanes()
        pairs = []
        for a in range(8):
            first = blocks[4 * a + 2 * half, rows, :].astype(F32)
            second = blocks[4 * a + 2 * half + 1, rows, :].astype(F32)
            pairs.append(
                (jnp.where(low, first, swap_halves(second)), jnp.where(low, swap_halves(first), second))
            )
        return pairs

    return load


def emit_fields(fields):
    def emit(block, rows, half, re, im):
        for a in range(8):
            fields[2 * a + half, 0, rows, :] = re[a]
            fields[2 * a + half, 1, rows, :] = im[a]

    return emit


def shuffle_fields(fields, back):
    lane = lax.broadcasted_iota(jnp.int32, (16, 128), 1)
    for column in range(16):
        parts = [fields[column, index % 2, 16 * (index // 2) : 16 * (index // 2) + 16, :] for index in range(8)]
        for bit, shift in ((4, 64), (2, 32), (1, 16)):
            low = lax.rem(lane // shift, 2) == 0
            for index in range(8):
                if index & bit == 0:
                    first, second = parts[index], parts[index + bit]
                    parts[index] = jnp.where(low, first, pltpu.roll(second, shift, 1))
                    parts[index + bit] = jnp.where(low, pltpu.roll(first, 128 - shift, 1), second)
        for index in range(8):
            back[index % 4, 2 * column + index // 4] = parts[index].astype(BF16)


def taps_of(position, places):
    distance = places - position
    inside = (distance > -4.0) & (distance <= 4.0)
    return jnp.where(inside, jnp.exp2(distance * distance * TAP_RATE), 0.0)


def place_index():
    place = lax.broadcasted_iota(jnp.int32, (TILE, V), 0)
    return (place // 8 + 8 * lax.rem(place, 8) - 3).astype(F32)


def grid_tile(tile, taps_u, taps_v, weight):
    partial = lax.dot_general(tile, taps_u, (((0,), (0,)), ((), ())), preferred_element_type=F32)
    real = jnp.sum(partial[0:64] * taps_v, axis=0, keepdims=True) * weight
    imag = jnp.sum(partial[64:128] * taps_v, axis=0, keepdims=True) * -weight
    spread = jnp.concatenate([taps_v * real, taps_v * imag], axis=0).astype(BF16)
    return lax.dot_general(taps_u, spread, (((1,), (1,)), ((), ())), preferred_element_type=F32).astype(BF16)


def chunk_rows(chunk):
    return pl.ds(pl.multiple_of(chunk * 16, 16), 16)


def send_all(axis, size, me, source, target, send, recv):
    def step(offset, carry):
        peer = lax.rem(me + offset, size)
        pltpu.make_async_remote_copy(
            source(peer), target, send, recv, device_id={axis: peer}, device_id_type=MESH
        ).start()
        return carry

    lax.fori_loop(1, size, step, 0)


def wait_recv(view, recv):
    pltpu.make_async_copy(view, view, recv).wait()


def greet(axis, size, me, barrier):
    def step(offset, carry):
        pl.semaphore_signal(
            barrier, inc=1, device_id={axis: lax.rem(me + offset, size)}, device_id_type=MESH
        )
        return carry

    lax.fori_loop(1, size, step, 0)


def send_planes(plane, terms, others, rows, send, recv):
    chip, core = plane // 2, lax.rem(plane, 2)
    for ahead, other in ((2, 0), (2, 1), (1, 0), (3, 0), (1, 1), (3, 1), (0, 1)):
        peer = lax.rem(chip + ahead, 4) * 2 + lax.rem(core + other, 2)
        pltpu.make_async_remote_copy(
            terms.at[peer, :, rows],
            others.at[plane, :, rows],
            send,
            recv,
            device_id={"plane": peer},
            device_id_type=MESH,
        ).start()


def whole_kernel(
    w_ref,
    owner_in,
    counts_in,
    image_in,
    positions_in,
    weights_in,
    table_in,
    twiddle_in,
    others,
    owner,
    counts,
    image,
    positions,
    weights,
    table,
    twiddle,
    packed,
    kept,
    got_packed,
    got_kept,
    stacked,
    blocks,
    got,
    tiles,
    gridded,
    back,
    got_back,
    middle,
    screen,
    terms,
    all_taps,
    tile_weight,
    fields,
    names,
    seconds,
    local_sem,
    vis_send,
    vis_recv,
    out_send,
    out_recv,
    back_send,
    back_recv,
    term_send,
    term_recv,
):
    me = lax.axis_index("row")
    plane = lax.axis_index("plane")
    barrier = pltpu.get_barrier_semaphore()
    greet("row", ROWS, me, barrier)
    greet("plane", PLANES, plane, barrier)
    loads = [
        pltpu.make_async_copy(source, target, local_sem.at[index])
        for index, (source, target) in enumerate(
            (
                (owner_in, owner),
                (counts_in, counts),
                (image_in, image),
                (twiddle_in, twiddle),
                (positions_in, positions),
                (weights_in, weights),
                (table_in, table),
            )
        )
    ]
    for copy in loads:
        copy.start()
    w = w_ref[0]

    def load(block, rows, half):
        pairs = []
        for a in range(8):
            col = 256 * a + 128 * half
            cosine, sine = screen[0, rows, col : col + 128], screen[1, rows, col : col + 128]
            real, imag = image[0, rows, col : col + 128], image[1, rows, col : col + 128]
            pairs.append((real * cosine + imag * sine, real * sine - imag * cosine))
        return pairs

    def prepare(block, carry):
        rows = chunk_rows(block)
        for piece in range(16):
            lanes = slice(128 * piece, 128 * piece + 128)
            cosine, sine = chunk_screen(w, me * 64 + block * 16, 128 * piece)
            screen[0, rows, lanes] = cosine
            screen[1, rows, lanes] = sine
        return carry

    lax.fori_loop(0, 4, prepare, 0)
    for copy in loads[0:6]:
        copy.wait()
    place_of = lax.broadcasted_iota(jnp.int32, (1, V), 1)
    for peer in range(ROWS):
        pair = slice(2 * peer, 2 * peer + 2)
        packed[peer] = positions[0, 0, pair, :] * 8192 + positions[0, 1, pair, :]
        chosen = []
        for item in range(2):
            slot = 2 * peer + item
            chosen.append(jnp.where(place_of < counts[0, slot], weights[0, slot : slot + 1, :], 0.0))
        kept[peer] = jnp.concatenate(chosen, axis=0).astype(BF16)

    def first_spread(block, carry):
        spread_block(load, block, twiddle, stacked)
        return carry

    lax.fori_loop(0, 4, first_spread, 0)
    pl.semaphore_wait(barrier, ROWS + PLANES - 2)
    send_all("row", ROWS, me, lambda peer: packed.at[peer], got_packed.at[me], vis_send.at[0], vis_recv.at[0])
    loads[6].wait()
    turn_blocks(stacked, table, blocks)

    def send_chunk(chunk, carry):
        rows = chunk_rows(chunk)
        send_all(
            "row", ROWS, me, lambda peer: blocks.at[peer, rows], got.at[me, rows], out_send.at[chunk], out_recv.at[chunk]
        )
        return carry

    lax.fori_loop(0, 4, send_chunk, 0)
    send_all("row", ROWS, me, lambda peer: kept.at[peer], got_kept.at[me], vis_send.at[1], vis_recv.at[1])
    got_packed[me] = packed[me]
    got_kept[me] = kept[me]
    got[me] = blocks[me]
    places = place_index()
    most = pl.ds(0, ROWS - 1)
    wait_recv(got_packed.at[most], vis_recv.at[0])

    def tap_step(item, carry):
        name = owner[me * ROWS + item]

        def count(other, total):
            return total + jnp.where((owner[me * ROWS + other] == name) & (other < item), 1, 0)

        second = lax.fori_loop(0, ROWS, count, 0, unroll=True) > 0
        names[item] = name
        seconds[item] = jnp.where(second, 1, 0)
        both = got_packed[name]
        place = jnp.where(second, both[1:2], both[0:1])
        u_part = place // 8192
        all_taps[item, 0] = taps_of(u_part.astype(F32) * (1.0 / OVER), places).astype(BF16)
        all_taps[item, 1] = taps_of((place - u_part * 8192).astype(F32) * (1.0 / OVER), places).astype(BF16)
        return carry

    lax.fori_loop(0, ROWS, tap_step, 0)
    load_got = load_received(got)

    def second_spread(chunk, carry):
        wait_recv(got.at[most, chunk_rows(chunk)], out_recv.at[chunk])
        spread_block(load_got, chunk, twiddle, stacked)
        return carry

    lax.fori_loop(0, 4, second_spread, 0)
    turn_blocks(stacked, table, tiles)

    wait_recv(got_kept.at[most], vis_recv.at[1])
    for group in range(0, ROWS, 8):
        pairs = [got_kept[names[item]].astype(F32) for item in range(group, group + 8)]
        picked = [jnp.where(seconds[group + item] > 0, pairs[item][1:2], pairs[item][0:1]) for item in range(8)]
        for item in range(8):
            tile_weight[group + item] = picked[item]

    def grid_step(group, carry):
        for place in range(16):
            item = group * 16 + place
            gridded[item] = grid_tile(
                tiles[item], all_taps[item, 0], all_taps[item, 1].astype(F32), tile_weight[item]
            )
        return carry

    lax.fori_loop(0, 2, grid_step, 0)
    for pair in range(4):
        gather_pair(pair, gridded, table, twiddle, middle)
    emit_back = emit_fields(fields)
    for block in range(4):
        last_block(block, middle, emit_back)
    shuffle_fields(fields, back)

    def back_send_one(peer, chunk):
        pltpu.make_async_remote_copy(
            back.at[chunk, peer],
            got_back.at[chunk, me],
            back_send.at[chunk],
            back_recv.at[chunk],
            device_id={"row": peer},
            device_id_type=MESH,
        ).start()

    for first, second, middle_z, late in ((((0, 1), (0,), (0,), ()), ((2, 3), (1, 2), (1,), (0,)), ((), (3,), (2,), (1,)), ((), (), (3,), (2, 3)))):

        def back_step(offset, carry, first=first, second=second, middle_z=middle_z, late=late):
            peer = lax.rem(me + offset, ROWS)
            for chunks, chosen in (
                (first, peer < 4),
                (second, (peer >= 4) & (peer < 8)),
                (middle_z, (peer >= 8) & (peer < 16)),
                (late, peer >= 16),
            ):
                if chunks:

                    @pl.when(chosen)
                    def _(chunks=chunks):
                        for chunk in chunks:
                            back_send_one(peer, chunk)

            return carry

        lax.fori_loop(1, ROWS, back_step, 0)
    for chunk in range(4):
        got_back[chunk, me] = back[chunk, me]

    def emit(block, rows, half, re, im):
        for a in range(8):
            lanes = slice(128 * half, 128 * half + 128)
            full = slice(256 * a + 128 * half, 256 * a + 128 * half + 128)
            cosine, sine = screen[0, rows, full], screen[1, rows, full]
            terms[a, 0, rows, lanes] = (re[a] * cosine - im[a] * sine).astype(BF16)
            terms[a, 1, rows, lanes] = (re[a] * sine + im[a] * cosine).astype(BF16)

    def term_chunk(chunk, carry):
        wait_recv(got_back.at[chunk, most], back_recv.at[chunk])
        gather_chunk(chunk, got_back, table, twiddle, middle)
        last_block(chunk, middle, emit)
        rows = chunk_rows(chunk)
        send_planes(plane, terms, others, rows, term_send, term_recv)
        return carry

    lax.fori_loop(0, 4, term_chunk, 0)
    mine = pltpu.make_async_copy(terms.at[plane], others.at[plane], local_sem.at[0])
    mine.start()
    wait_recv(packed.at[most], vis_send.at[0])
    wait_recv(kept.at[most], vis_send.at[1])
    for chunk in range(4):
        wait_recv(blocks.at[most, chunk_rows(chunk)], out_send.at[chunk])
        wait_recv(back.at[chunk, most], back_send.at[chunk])
    mine.wait()
    rest = pl.ds(0, PLANES - 1)
    wait_recv(terms.at[rest], term_send)
    wait_recv(others.at[rest], term_recv)


def local(image, w_planes, owner, positions, weights, counts):
    table, twiddle = host_tables()
    smem = pl.BlockSpec(memory_space=pltpu.SMEM)
    anywhere = pl.BlockSpec(memory_space=pl.ANY)
    dma = pltpu.SemaphoreType.DMA
    block = pltpu.VMEM((ROWS, TILE, 128), BF16)
    others = pl.pallas_call(
        whole_kernel,
        out_shape=jax.ShapeDtypeStruct((PLANES, 2, 64, 256), BF16),
        in_specs=[smem] + [pl.BlockSpec(memory_space=pltpu.HBM)] * 7,
        out_specs=anywhere,
        scratch_shapes=[
            pltpu.SMEM((ROWS * ROWS,), jnp.int32),
            pltpu.SMEM((1, 64), jnp.int32),
            pltpu.VMEM((2, 64, EXTENT), F32),
            pltpu.VMEM((1, 2, 64, V), jnp.int32),
            pltpu.VMEM((1, 64, V), F32),
            pltpu.VMEM((512, 512), BF16),
            pltpu.VMEM((2, 8, 256), F32),
            pltpu.VMEM((ROWS, 2, V), jnp.int32),
            pltpu.VMEM((ROWS, 2, V), BF16),
            pltpu.VMEM((ROWS, 2, V), jnp.int32),
            pltpu.VMEM((ROWS, 2, V), BF16),
            pltpu.VMEM((8, 64, 512), BF16),
            block,
            block,
            block,
            block,
            pltpu.VMEM((4, ROWS, 16, 128), BF16),
            pltpu.VMEM((4, ROWS, 16, 128), BF16),
            pltpu.VMEM((8, 64, 512), F32),
            pltpu.VMEM((2, 64, EXTENT), F32),
            pltpu.VMEM((PLANES, 2, 64, 256), BF16),
            pltpu.VMEM((ROWS, 2, TILE, V), BF16),
            pltpu.VMEM((ROWS, 1, V), F32),
            pltpu.VMEM((16, 2, 64, 128), F32),
            pltpu.SMEM((ROWS,), jnp.int32),
            pltpu.SMEM((ROWS,), jnp.int32),
            dma((7,)),
            dma((2,)),
            dma((2,)),
            dma((4,)),
            dma((4,)),
            dma((4,)),
            dma((4,)),
            dma,
            dma,
        ],
        compiler_params=pltpu.CompilerParams(collective_id=0, has_side_effects=True, vmem_limit_bytes=24 * 1024 * 1024),
        name="whole",
    )(
        w_planes,
        *[
            pltpu.with_memory_space_constraint(value, pltpu.HBM)
            for value in (
                owner.reshape(-1),
                counts,
                image,
                positions,
                weights,
                jnp.asarray(table),
                jnp.asarray(twiddle),
            )
        ],
    )
    return jnp.sum(others.astype(F32), axis=0)


def solution(mesh):
    in_specs = (
        P(None, "row", None),
        P("plane"),
        P("plane", None, None),
        P("plane", None, "row", None),
        P("plane", "row", None),
        P("plane", "row"),
    )
    out_specs = P(None, "row", "plane")
    return jax.shard_map(local, mesh=mesh, in_specs=in_specs, out_specs=out_specs, check_vma=False)
```

```python
import functools

import jax
import jax.numpy as jnp
import ml_dtypes
import numpy as np
from jax import lax
from jax.experimental import pallas as pl
from jax.experimental.pallas import tpu as pltpu
from jax.sharding import PartitionSpec as P

TILE = 64
S = 8
OVER = 128
V = 256
FIELD_SPAN = 0.7
EXTENT = 2048
ROWS = 32
PLANES = 8
SCALE = 1.0 / 2048.0
TAP_RATE = -4.0 * 1.4426950408889634
MESH = pl.DeviceIdType.MESH
F32 = jnp.float32
BF16 = jnp.bfloat16
ROOT = 0.7071067811865476
SIN_POLY = (6.283184916495429, -41.34158923268831, 81.59994332977428, -76.61447253115396, 41.342882354135696, -12.471243534350362)
COS_POLY = (0.9999999890590228, -19.739204499453827, 64.9391174598908, -85.45013953079768, 60.16763095026347, -25.967599245923736, 6.52865815775625)


def host_tables():
    index = np.arange(256)
    angle = 2.0 * np.pi / 256.0 * (index[:, None] * index[None, :] % 256)
    cosine, sine = np.cos(angle), np.sin(angle)
    table = np.block([[cosine, sine], [-sine, cosine]]).astype(ml_dtypes.bfloat16)
    turn = 2.0 * np.pi / 2048.0 * (np.arange(8)[:, None] * index[None, :])
    return table, np.stack([np.cos(turn), np.sin(turn)]).astype(np.float32)


def dft4(re, im):
    ar, ai, br, bi = re[0] + re[2], im[0] + im[2], re[0] - re[2], im[0] - im[2]
    cr, ci, dr, di = re[1] + re[3], im[1] + im[3], re[1] - re[3], im[1] - im[3]
    return [ar + cr, br - di, ar - cr, br + di], [ai + ci, bi + dr, ai - ci, bi - dr]


def dft8(re, im):
    er, ei = dft4(re[0::2], im[0::2])
    od, oi = dft4(re[1::2], im[1::2])
    tr = [od[0], (od[1] - oi[1]) * ROOT, -oi[2], (od[3] + oi[3]) * -ROOT]
    ti = [oi[0], (od[1] + oi[1]) * ROOT, od[2], (od[3] - oi[3]) * ROOT]
    return [er[k] + tr[k] for k in range(4)] + [er[k] - tr[k] for k in range(4)], [
        ei[k] + ti[k] for k in range(4)
    ] + [ei[k] - ti[k] for k in range(4)]


def swap_halves(value):
    return pltpu.roll(value, 64, 1)


def screen_of(turns):
    part = turns - jnp.round(turns)
    square = part * part
    sine = jnp.full_like(part, SIN_POLY[-1])
    for term in SIN_POLY[-2::-1]:
        sine = sine * square + term
    cosine = jnp.full_like(part, COS_POLY[-1])
    for term in COS_POLY[-2::-1]:
        cosine = cosine * square + term
    return cosine * SCALE, sine * part * SCALE


def chunk_screen(w, row_start, col_start):
    spacing = FIELD_SPAN / EXTENT
    rows = lax.broadcasted_iota(jnp.int32, (16, 128), 0) + (row_start - EXTENT // 2)
    cols = lax.broadcasted_iota(jnp.int32, (16, 128), 1) + (col_start - EXTENT // 2)
    rows = rows.astype(F32) * spacing
    cols = cols.astype(F32) * spacing
    elevation = jnp.sqrt(1.0 - rows * rows - cols * cols) - 1.0
    return screen_of(w * elevation)


def spread_block(load, block, twiddle, stacked):
    rows = pl.ds(pl.multiple_of(block * 16, 16), 16)
    for half in range(2):
        pairs = load(block, rows, half)
        re, im = dft8([pair[0] for pair in pairs], [pair[1] for pair in pairs])
        lanes = slice(128 * half, 128 * half + 128)
        other = slice(256 + 128 * half, 384 + 128 * half)
        for q in range(8):
            if q == 0:
                real, imag = re[0], im[0]
            else:
                cosine, sine = twiddle[0, q : q + 1, lanes], twiddle[1, q : q + 1, lanes]
                real, imag = re[q] * cosine - im[q] * sine, re[q] * sine + im[q] * cosine
            stacked[q, rows, lanes] = real.astype(BF16)
            stacked[q, rows, other] = imag.astype(BF16)


def turn_blocks(stacked, table, blocks):
    matrix = table[...]
    for pair in range(4):
        left = stacked[2 * pair : 2 * pair + 2].reshape(128, 512)
        out = jnp.dot(left, matrix, preferred_element_type=F32)
        for half in range(2):
            real, imag = slice(128 * half, 128 * half + 128), slice(256 + 128 * half, 384 + 128 * half)
            turned = []
            for item in range(2):
                rows = slice(64 * item, 64 * item + 64)
                square = jnp.concatenate([out[rows, real], out[rows, imag]], axis=0)
                turned.append(jnp.transpose(square).reshape(16, 8, 128))
            both = jnp.concatenate(turned, axis=1).astype(BF16)
            blocks[16 * half : 16 * half + 16, 16 * pair : 16 * pair + 16, :] = both


def gather_pair(pair, blocks, table, twiddle, middle):
    matrix = table[...]
    rows = blocks[:, pl.ds(pl.multiple_of(16 * pair, 16), 16), :].astype(F32)
    for item in range(2):
        q = 2 * pair + item
        flat = rows[:, 8 * item : 8 * item + 8, :].reshape(256, 128)
        low = jnp.transpose(flat[0:128]).astype(BF16)
        high = jnp.transpose(flat[128:256]).astype(BF16)
        left = jnp.concatenate([low[0:64], high[0:64], low[64:128], high[64:128]], axis=1)
        out = jnp.dot(left, matrix, preferred_element_type=F32)
        real, imag = out[:, 0:256], out[:, 256:512]
        cosine, sine = twiddle[0, pl.ds(q, 1), :], twiddle[1, pl.ds(q, 1), :]
        middle[q, :, 0:256] = real * cosine - imag * sine
        middle[q, :, 256:512] = real * sine + imag * cosine


def gather_chunk(chunk, blocks, table, twiddle, middle):
    values = blocks[chunk].astype(F32)
    left = []
    for item in range(2):
        flat = values[:, 8 * item : 8 * item + 8, :].reshape(256, 128)
        low = jnp.transpose(flat[0:128]).reshape(4, 2, 16, 128)
        high = jnp.transpose(flat[128:256]).reshape(4, 2, 16, 128)
        parts = [low[:, 0], high[:, 0], low[:, 1], high[:, 1]]
        left.append(jnp.concatenate([part.reshape(64, 128) for part in parts], axis=1))
    out = jnp.dot(jnp.concatenate(left, axis=0).astype(BF16), table[...], preferred_element_type=F32)
    rows = chunk_rows(chunk)
    for item in range(2):
        for place in range(4):
            q = 2 * place + item
            piece = out[64 * item + 16 * place : 64 * item + 16 * place + 16]
            real, imag = piece[:, 0:256], piece[:, 256:512]
            if q:
                cosine, sine = twiddle[0, q : q + 1, :], twiddle[1, q : q + 1, :]
                real, imag = real * cosine - imag * sine, real * sine + imag * cosine
            middle[q, rows, 0:256] = real
            middle[q, rows, 256:512] = imag


def last_block(block, middle, emit):
    rows = pl.ds(pl.multiple_of(block * 16, 16), 16)
    for half in range(2):
        lanes = slice(128 * half, 128 * half + 128)
        other = slice(256 + 128 * half, 384 + 128 * half)
        re, im = dft8([middle[q, rows, lanes] for q in range(8)], [middle[q, rows, other] for q in range(8)])
        emit(block, rows, half, re, im)


def low_lanes():
    return lax.broadcasted_iota(jnp.int32, (16, 128), 1) < 64


def load_received(blocks):
    def load(block, rows, half):
        low = low_lanes()
        pairs = []
        for a in range(8):
            first = blocks[4 * a + 2 * half, rows, :].astype(F32)
            second = blocks[4 * a + 2 * half + 1, rows, :].astype(F32)
            pairs.append(
                (jnp.where(low, first, swap_halves(second)), jnp.where(low, swap_halves(first), second))
            )
        return pairs

    return load


def emit_fields(fields):
    def emit(block, rows, half, re, im):
        for a in range(8):
            fields[2 * a + half, 0, rows, :] = re[a]
            fields[2 * a + half, 1, rows, :] = im[a]

    return emit


def shuffle_fields(fields, back):
    lane = lax.broadcasted_iota(jnp.int32, (16, 128), 1)
    for column in range(16):
        parts = [fields[column, index % 2, 16 * (index // 2) : 16 * (index // 2) + 16, :] for index in range(8)]
        for bit, shift in ((4, 64), (2, 32), (1, 16)):
            low = lax.rem(lane // shift, 2) == 0
            for index in range(8):
                if index & bit == 0:
                    first, second = parts[index], parts[index + bit]
                    parts[index] = jnp.where(low, first, pltpu.roll(second, shift, 1))
                    parts[index + bit] = jnp.where(low, pltpu.roll(first, 128 - shift, 1), second)
        for index in range(8):
            back[index % 4, 2 * column + index // 4] = parts[index].astype(BF16)


def taps_of(position, places):
    distance = places - position
    inside = (distance > -4.0) & (distance <= 4.0)
    return jnp.where(inside, jnp.exp2(distance * distance * TAP_RATE), 0.0)


def place_index():
    place = lax.broadcasted_iota(jnp.int32, (TILE, V), 0)
    return (place // 8 + 8 * lax.rem(place, 8) - 3).astype(F32)


def grid_tile(tile, taps_u, taps_v, weight):
    partial = lax.dot_general(tile, taps_u, (((0,), (0,)), ((), ())), preferred_element_type=F32)
    real = jnp.sum(partial[0:64] * taps_v, axis=0, keepdims=True) * weight
    imag = jnp.sum(partial[64:128] * taps_v, axis=0, keepdims=True) * -weight
    spread = jnp.concatenate([taps_v * real, taps_v * imag], axis=0).astype(BF16)
    return lax.dot_general(taps_u, spread, (((1,), (1,)), ((), ())), preferred_element_type=F32).astype(BF16)


def chunk_rows(chunk):
    return pl.ds(pl.multiple_of(chunk * 16, 16), 16)


def send_all(axis, size, me, source, target, send, recv):
    def step(offset, carry):
        peer = lax.rem(me + offset, size)
        pltpu.make_async_remote_copy(
            source(peer), target, send, recv, device_id={axis: peer}, device_id_type=MESH
        ).start()
        return carry

    lax.fori_loop(1, size, step, 0)


def wait_recv(view, recv):
    pltpu.make_async_copy(view, view, recv).wait()


def greet(axis, size, me, barrier):
    def step(index, carry):
        ahead = size // 2 + jnp.where(lax.rem(index, 2) == 1, -((index + 1) // 2), index // 2)
        pl.semaphore_signal(
            barrier, inc=1, device_id={axis: lax.rem(me + ahead, size)}, device_id_type=MESH
        )
        return carry

    lax.fori_loop(0, size - 1, step, 0)


def send_planes(plane, terms, others, rows, send, recv):
    chip, core = plane // 2, lax.rem(plane, 2)
    for ahead, other in ((2, 0), (2, 1), (1, 0), (3, 0), (1, 1), (3, 1), (0, 1)):
        peer = lax.rem(chip + ahead, 4) * 2 + lax.rem(core + other, 2)
        pltpu.make_async_remote_copy(
            terms.at[peer, :, rows],
            others.at[plane, :, rows],
            send,
            recv,
            device_id={"plane": peer},
            device_id_type=MESH,
        ).start()


def whole_kernel(
    w_ref,
    owner_in,
    counts_in,
    image_in,
    positions_in,
    weights_in,
    table_in,
    twiddle_in,
    others,
    owner,
    counts,
    image,
    positions,
    weights,
    table,
    twiddle,
    packed,
    kept,
    got_packed,
    got_kept,
    stacked,
    blocks,
    got,
    tiles,
    gridded,
    back,
    got_back,
    middle,
    screen,
    terms,
    all_taps,
    tile_weight,
    fields,
    names,
    seconds,
    local_sem,
    vis_send,
    vis_recv,
    out_send,
    out_recv,
    back_send,
    back_recv,
    term_send,
    term_recv,
):
    me = lax.axis_index("row")
    plane = lax.axis_index("plane")
    barrier = pltpu.get_barrier_semaphore()
    greet("row", ROWS, me, barrier)
    greet("plane", PLANES, plane, barrier)
    loads = [
        pltpu.make_async_copy(source, target, local_sem.at[index])
        for index, (source, target) in enumerate(
            (
                (owner_in, owner),
                (counts_in, counts),
                (image_in, image),
                (twiddle_in, twiddle),
                (positions_in, positions),
                (weights_in, weights),
                (table_in, table),
            )
        )
    ]
    for copy in loads:
        copy.start()
    w = w_ref[0]

    def load(block, rows, half):
        pairs = []
        for a in range(8):
            col = 256 * a + 128 * half
            cosine, sine = screen[0, rows, col : col + 128], screen[1, rows, col : col + 128]
            real, imag = image[0, rows, col : col + 128], image[1, rows, col : col + 128]
            pairs.append((real * cosine + imag * sine, real * sine - imag * cosine))
        return pairs

    def prepare(block, carry):
        rows = chunk_rows(block)
        for piece in range(16):
            lanes = slice(128 * piece, 128 * piece + 128)
            cosine, sine = chunk_screen(w, me * 64 + block * 16, 128 * piece)
            screen[0, rows, lanes] = cosine
            screen[1, rows, lanes] = sine
        return carry

    lax.fori_loop(0, 4, prepare, 0)
    for copy in loads[0:6]:
        copy.wait()
    place_of = lax.broadcasted_iota(jnp.int32, (1, V), 1)
    for peer in range(ROWS):
        pair = slice(2 * peer, 2 * peer + 2)
        packed[peer] = positions[0, 0, pair, :] * 8192 + positions[0, 1, pair, :]
        chosen = []
        for item in range(2):
            slot = 2 * peer + item
            chosen.append(jnp.where(place_of < counts[0, slot], weights[0, slot : slot + 1, :], 0.0))
        kept[peer] = jnp.concatenate(chosen, axis=0).astype(BF16)

    def first_spread(block, carry):
        spread_block(load, block, twiddle, stacked)
        return carry

    lax.fori_loop(0, 4, first_spread, 0)
    pl.semaphore_wait(barrier, ROWS + PLANES - 2)
    send_all("row", ROWS, me, lambda peer: packed.at[peer], got_packed.at[me], vis_send.at[0], vis_recv.at[0])
    loads[6].wait()
    turn_blocks(stacked, table, blocks)

    def send_chunk(chunk, carry):
        rows = chunk_rows(chunk)
        send_all(
            "row", ROWS, me, lambda peer: blocks.at[peer, rows], got.at[me, rows], out_send.at[chunk], out_recv.at[chunk]
        )
        return carry

    lax.fori_loop(0, 4, send_chunk, 0)
    send_all("row", ROWS, me, lambda peer: kept.at[peer], got_kept.at[me], vis_send.at[1], vis_recv.at[1])
    got_packed[me] = packed[me]
    got_kept[me] = kept[me]
    got[me] = blocks[me]
    places = place_index()
    most = pl.ds(0, ROWS - 1)
    wait_recv(got_packed.at[most], vis_recv.at[0])

    def tap_step(item, carry):
        name = owner[me * ROWS + item]

        def count(other, total):
            return total + jnp.where((owner[me * ROWS + other] == name) & (other < item), 1, 0)

        second = lax.fori_loop(0, ROWS, count, 0, unroll=True) > 0
        names[item] = name
        seconds[item] = jnp.where(second, 1, 0)
        both = got_packed[name]
        place = jnp.where(second, both[1:2], both[0:1])
        u_part = place // 8192
        all_taps[item, 0] = taps_of(u_part.astype(F32) * (1.0 / OVER), places).astype(BF16)
        all_taps[item, 1] = taps_of((place - u_part * 8192).astype(F32) * (1.0 / OVER), places).astype(BF16)
        return carry

    lax.fori_loop(0, ROWS, tap_step, 0)
    load_got = load_received(got)

    def second_spread(chunk, carry):
        wait_recv(got.at[most, chunk_rows(chunk)], out_recv.at[chunk])
        spread_block(load_got, chunk, twiddle, stacked)
        return carry

    lax.fori_loop(0, 4, second_spread, 0)
    turn_blocks(stacked, table, tiles)

    wait_recv(got_kept.at[most], vis_recv.at[1])
    for group in range(0, ROWS, 8):
        pairs = [got_kept[names[item]].astype(F32) for item in range(group, group + 8)]
        picked = [jnp.where(seconds[group + item] > 0, pairs[item][1:2], pairs[item][0:1]) for item in range(8)]
        for item in range(8):
            tile_weight[group + item] = picked[item]

    def grid_step(group, carry):
        for place in range(16):
            item = group * 16 + place
            gridded[item] = grid_tile(
                tiles[item], all_taps[item, 0], all_taps[item, 1].astype(F32), tile_weight[item]
            )
        return carry

    lax.fori_loop(0, 2, grid_step, 0)
    for pair in range(4):
        gather_pair(pair, gridded, table, twiddle, middle)
    emit_back = emit_fields(fields)
    for block in range(4):
        last_block(block, middle, emit_back)
    shuffle_fields(fields, back)

    def back_send_one(peer, chunk):
        pltpu.make_async_remote_copy(
            back.at[chunk, peer],
            got_back.at[chunk, me],
            back_send.at[chunk],
            back_recv.at[chunk],
            device_id={"row": peer},
            device_id_type=MESH,
        ).start()

    for first, second, middle_z, late in ((((0, 1), (0,), (0,), ()), ((2, 3), (1, 2), (1,), (0,)), ((), (3,), (2, 3), (1, 2)), ((), (), (), (3,)))):

        def back_step(offset, carry, first=first, second=second, middle_z=middle_z, late=late):
            peer = lax.rem(me + offset, ROWS)
            for chunks, chosen in (
                (first, peer < 4),
                (second, (peer >= 4) & (peer < 8)),
                (middle_z, (peer >= 8) & (peer < 16)),
                (late, peer >= 16),
            ):
                if chunks:

                    @pl.when(chosen)
                    def _(chunks=chunks):
                        for chunk in chunks:
                            back_send_one(peer, chunk)

            return carry

        lax.fori_loop(1, ROWS, back_step, 0)
    for chunk in range(4):
        got_back[chunk, me] = back[chunk, me]

    def emit(block, rows, half, re, im):
        for a in range(8):
            lanes = slice(128 * half, 128 * half + 128)
            full = slice(256 * a + 128 * half, 256 * a + 128 * half + 128)
            cosine, sine = screen[0, rows, full], screen[1, rows, full]
            terms[a, 0, rows, lanes] = (re[a] * cosine - im[a] * sine).astype(BF16)
            terms[a, 1, rows, lanes] = (re[a] * sine + im[a] * cosine).astype(BF16)

    def term_chunk(chunk, carry):
        wait_recv(got_back.at[chunk, most], back_recv.at[chunk])
        gather_chunk(chunk, got_back, table, twiddle, middle)
        last_block(chunk, middle, emit)
        rows = chunk_rows(chunk)
        send_planes(plane, terms, others, rows, term_send, term_recv)
        return carry

    lax.fori_loop(0, 4, term_chunk, 0)
    mine = pltpu.make_async_copy(terms.at[plane], others.at[plane], local_sem.at[0])
    mine.start()
    wait_recv(packed.at[most], vis_send.at[0])
    wait_recv(kept.at[most], vis_send.at[1])
    for chunk in range(4):
        wait_recv(blocks.at[most, chunk_rows(chunk)], out_send.at[chunk])
        wait_recv(back.at[chunk, most], back_send.at[chunk])
    mine.wait()
    rest = pl.ds(0, PLANES - 1)
    wait_recv(terms.at[rest], term_send)
    wait_recv(others.at[rest], term_recv)


def local(image, w_planes, owner, positions, weights, counts):
    table, twiddle = host_tables()
    smem = pl.BlockSpec(memory_space=pltpu.SMEM)
    anywhere = pl.BlockSpec(memory_space=pl.ANY)
    dma = pltpu.SemaphoreType.DMA
    block = pltpu.VMEM((ROWS, TILE, 128), BF16)
    others = pl.pallas_call(
        whole_kernel,
        out_shape=jax.ShapeDtypeStruct((PLANES, 2, 64, 256), BF16),
        in_specs=[smem] + [pl.BlockSpec(memory_space=pltpu.HBM)] * 7,
        out_specs=anywhere,
        scratch_shapes=[
            pltpu.SMEM((ROWS * ROWS,), jnp.int32),
            pltpu.SMEM((1, 64), jnp.int32),
            pltpu.VMEM((2, 64, EXTENT), F32),
            pltpu.VMEM((1, 2, 64, V), jnp.int32),
            pltpu.VMEM((1, 64, V), F32),
            pltpu.VMEM((512, 512), BF16),
            pltpu.VMEM((2, 8, 256), F32),
            pltpu.VMEM((ROWS, 2, V), jnp.int32),
            pltpu.VMEM((ROWS, 2, V), BF16),
            pltpu.VMEM((ROWS, 2, V), jnp.int32),
            pltpu.VMEM((ROWS, 2, V), BF16),
            pltpu.VMEM((8, 64, 512), BF16),
            block,
            block,
            block,
            block,
            pltpu.VMEM((4, ROWS, 16, 128), BF16),
            pltpu.VMEM((4, ROWS, 16, 128), BF16),
            pltpu.VMEM((8, 64, 512), F32),
            pltpu.VMEM((2, 64, EXTENT), F32),
            pltpu.VMEM((PLANES, 2, 64, 256), BF16),
            pltpu.VMEM((ROWS, 2, TILE, V), BF16),
            pltpu.VMEM((ROWS, 1, V), F32),
            pltpu.VMEM((16, 2, 64, 128), F32),
            pltpu.SMEM((ROWS,), jnp.int32),
            pltpu.SMEM((ROWS,), jnp.int32),
            dma((7,)),
            dma((2,)),
            dma((2,)),
            dma((4,)),
            dma((4,)),
            dma((4,)),
            dma((4,)),
            dma,
            dma,
        ],
        compiler_params=pltpu.CompilerParams(collective_id=0, has_side_effects=True, vmem_limit_bytes=24 * 1024 * 1024),
        name="whole",
    )(
        w_planes,
        *[
            pltpu.with_memory_space_constraint(value, pltpu.HBM)
            for value in (
                owner.reshape(-1),
                counts,
                image,
                positions,
                weights,
                jnp.asarray(table),
                jnp.asarray(twiddle),
            )
        ],
    )
    return jnp.sum(others.astype(F32), axis=0)


def solution(mesh):
    in_specs = (
        P(None, "row", None),
        P("plane"),
        P("plane", None, None),
        P("plane", None, "row", None),
        P("plane", "row", None),
        P("plane", "row"),
    )
    out_specs = P(None, "row", "plane")
    return jax.shard_map(local, mesh=mesh, in_specs=in_specs, out_specs=out_specs, check_vma=False)
```

```python
import functools

import jax
import jax.numpy as jnp
import ml_dtypes
import numpy as np
from jax import lax
from jax.experimental import pallas as pl
from jax.experimental.pallas import tpu as pltpu
from jax.sharding import PartitionSpec as P

TILE = 64
S = 8
OVER = 128
V = 256
FIELD_SPAN = 0.7
EXTENT = 2048
ROWS = 32
PLANES = 8
SCALE = 1.0 / 2048.0
TAP_RATE = -4.0 * 1.4426950408889634
MESH = pl.DeviceIdType.MESH
F32 = jnp.float32
BF16 = jnp.bfloat16
ROOT = 0.7071067811865476
SIN_POLY = (6.283184916495429, -41.34158923268831, 81.59994332977428, -76.61447253115396, 41.342882354135696, -12.471243534350362)
COS_POLY = (0.9999999890590228, -19.739204499453827, 64.9391174598908, -85.45013953079768, 60.16763095026347, -25.967599245923736, 6.52865815775625)


def host_tables():
    index = np.arange(256)
    angle = 2.0 * np.pi / 256.0 * (index[:, None] * index[None, :] % 256)
    cosine, sine = np.cos(angle), np.sin(angle)
    table = np.block([[cosine, sine], [-sine, cosine]]).astype(ml_dtypes.bfloat16)
    turn = 2.0 * np.pi / 2048.0 * (np.arange(8)[:, None] * index[None, :])
    return table, np.stack([np.cos(turn), np.sin(turn)]).astype(np.float32)


def dft4(re, im):
    ar, ai, br, bi = re[0] + re[2], im[0] + im[2], re[0] - re[2], im[0] - im[2]
    cr, ci, dr, di = re[1] + re[3], im[1] + im[3], re[1] - re[3], im[1] - im[3]
    return [ar + cr, br - di, ar - cr, br + di], [ai + ci, bi + dr, ai - ci, bi - dr]


def dft8(re, im):
    er, ei = dft4(re[0::2], im[0::2])
    od, oi = dft4(re[1::2], im[1::2])
    tr = [od[0], (od[1] - oi[1]) * ROOT, -oi[2], (od[3] + oi[3]) * -ROOT]
    ti = [oi[0], (od[1] + oi[1]) * ROOT, od[2], (od[3] - oi[3]) * ROOT]
    return [er[k] + tr[k] for k in range(4)] + [er[k] - tr[k] for k in range(4)], [
        ei[k] + ti[k] for k in range(4)
    ] + [ei[k] - ti[k] for k in range(4)]


def swap_halves(value):
    return pltpu.roll(value, 64, 1)


def screen_of(turns):
    part = turns - jnp.round(turns)
    square = part * part
    sine = jnp.full_like(part, SIN_POLY[-1])
    for term in SIN_POLY[-2::-1]:
        sine = sine * square + term
    cosine = jnp.full_like(part, COS_POLY[-1])
    for term in COS_POLY[-2::-1]:
        cosine = cosine * square + term
    return cosine * SCALE, sine * part * SCALE


def chunk_screen(w, row_start, col_start):
    spacing = FIELD_SPAN / EXTENT
    rows = lax.broadcasted_iota(jnp.int32, (16, 128), 0) + (row_start - EXTENT // 2)
    cols = lax.broadcasted_iota(jnp.int32, (16, 128), 1) + (col_start - EXTENT // 2)
    rows = rows.astype(F32) * spacing
    cols = cols.astype(F32) * spacing
    elevation = jnp.sqrt(1.0 - rows * rows - cols * cols) - 1.0
    return screen_of(w * elevation)


def spread_block(load, block, twiddle, stacked):
    rows = pl.ds(pl.multiple_of(block * 16, 16), 16)
    for half in range(2):
        pairs = load(block, rows, half)
        re, im = dft8([pair[0] for pair in pairs], [pair[1] for pair in pairs])
        lanes = slice(128 * half, 128 * half + 128)
        other = slice(256 + 128 * half, 384 + 128 * half)
        for q in range(8):
            if q == 0:
                real, imag = re[0], im[0]
            else:
                cosine, sine = twiddle[0, q : q + 1, lanes], twiddle[1, q : q + 1, lanes]
                real, imag = re[q] * cosine - im[q] * sine, re[q] * sine + im[q] * cosine
            stacked[q, rows, lanes] = real.astype(BF16)
            stacked[q, rows, other] = imag.astype(BF16)


def turn_blocks(stacked, table, blocks):
    matrix = table[...]
    for pair in range(4):
        left = stacked[2 * pair : 2 * pair + 2].reshape(128, 512)
        out = jnp.dot(left, matrix, preferred_element_type=F32)
        for half in range(2):
            real, imag = slice(128 * half, 128 * half + 128), slice(256 + 128 * half, 384 + 128 * half)
            turned = []
            for item in range(2):
                rows = slice(64 * item, 64 * item + 64)
                square = jnp.concatenate([out[rows, real], out[rows, imag]], axis=0)
                turned.append(jnp.transpose(square).reshape(16, 8, 128))
            both = jnp.concatenate(turned, axis=1).astype(BF16)
            blocks[16 * half : 16 * half + 16, 16 * pair : 16 * pair + 16, :] = both


def gather_pair(pair, blocks, table, twiddle, middle):
    matrix = table[...]
    rows = blocks[:, pl.ds(pl.multiple_of(16 * pair, 16), 16), :].astype(F32)
    for item in range(2):
        q = 2 * pair + item
        flat = rows[:, 8 * item : 8 * item + 8, :].reshape(256, 128)
        low = jnp.transpose(flat[0:128]).astype(BF16)
        high = jnp.transpose(flat[128:256]).astype(BF16)
        left = jnp.concatenate([low[0:64], high[0:64], low[64:128], high[64:128]], axis=1)
        out = jnp.dot(left, matrix, preferred_element_type=F32)
        real, imag = out[:, 0:256], out[:, 256:512]
        cosine, sine = twiddle[0, pl.ds(q, 1), :], twiddle[1, pl.ds(q, 1), :]
        middle[q, :, 0:256] = real * cosine - imag * sine
        middle[q, :, 256:512] = real * sine + imag * cosine


def gather_chunk(chunk, blocks, table, twiddle, middle):
    values = blocks[chunk].astype(F32)
    left = []
    for item in range(2):
        flat = values[:, 8 * item : 8 * item + 8, :].reshape(256, 128)
        low = jnp.transpose(flat[0:128]).reshape(4, 2, 16, 128)
        high = jnp.transpose(flat[128:256]).reshape(4, 2, 16, 128)
        parts = [low[:, 0], high[:, 0], low[:, 1], high[:, 1]]
        left.append(jnp.concatenate([part.reshape(64, 128) for part in parts], axis=1))
    out = jnp.dot(jnp.concatenate(left, axis=0).astype(BF16), table[...], preferred_element_type=F32)
    rows = chunk_rows(chunk)
    for item in range(2):
        for place in range(4):
            q = 2 * place + item
            piece = out[64 * item + 16 * place : 64 * item + 16 * place + 16]
            real, imag = piece[:, 0:256], piece[:, 256:512]
            if q:
                cosine, sine = twiddle[0, q : q + 1, :], twiddle[1, q : q + 1, :]
                real, imag = real * cosine - imag * sine, real * sine + imag * cosine
            middle[q, rows, 0:256] = real
            middle[q, rows, 256:512] = imag


def last_block(block, middle, emit):
    rows = pl.ds(pl.multiple_of(block * 16, 16), 16)
    for half in range(2):
        lanes = slice(128 * half, 128 * half + 128)
        other = slice(256 + 128 * half, 384 + 128 * half)
        re, im = dft8([middle[q, rows, lanes] for q in range(8)], [middle[q, rows, other] for q in range(8)])
        emit(block, rows, half, re, im)


def low_lanes():
    return lax.broadcasted_iota(jnp.int32, (16, 128), 1) < 64


def load_received(blocks):
    def load(block, rows, half):
        low = low_lanes()
        pairs = []
        for a in range(8):
            first = blocks[4 * a + 2 * half, rows, :].astype(F32)
            second = blocks[4 * a + 2 * half + 1, rows, :].astype(F32)
            pairs.append(
                (jnp.where(low, first, swap_halves(second)), jnp.where(low, swap_halves(first), second))
            )
        return pairs

    return load


def emit_fields(fields):
    def emit(block, rows, half, re, im):
        for a in range(8):
            fields[2 * a + half, 0, rows, :] = re[a].astype(BF16)
            fields[2 * a + half, 1, rows, :] = im[a].astype(BF16)

    return emit


def shuffle_fields(fields, back):
    lane = lax.broadcasted_iota(jnp.int32, (16, 128), 1)
    for column in range(16):
        parts = [fields[column, index % 2, 16 * (index // 2) : 16 * (index // 2) + 16, :] for index in range(8)]
        for bit, shift in ((4, 64), (2, 32), (1, 16)):
            low = lax.rem(lane // shift, 2) == 0
            for index in range(8):
                if index & bit == 0:
                    first, second = parts[index], parts[index + bit]
                    parts[index] = jnp.where(low, first, pltpu.roll(second, shift, 1))
                    parts[index + bit] = jnp.where(low, pltpu.roll(first, 128 - shift, 1), second)
        for index in range(8):
            back[index % 4, 2 * column + index // 4] = parts[index]


def taps_of(position, places):
    distance = places - position
    inside = (distance > -4.0) & (distance <= 4.0)
    return jnp.where(inside, jnp.exp2(distance * distance * TAP_RATE), 0.0)


def place_index():
    place = lax.broadcasted_iota(jnp.int32, (TILE, V), 0)
    return (place // 8 + 8 * lax.rem(place, 8) - 3).astype(F32)


def grid_tile(tile, taps_u, taps_v, weight):
    partial = lax.dot_general(tile, taps_u, (((0,), (0,)), ((), ())), preferred_element_type=F32)
    real = jnp.sum(partial[0:64] * taps_v, axis=0, keepdims=True) * weight
    imag = jnp.sum(partial[64:128] * taps_v, axis=0, keepdims=True) * -weight
    spread = jnp.concatenate([taps_v * real, taps_v * imag], axis=0).astype(BF16)
    return lax.dot_general(taps_u, spread, (((1,), (1,)), ((), ())), preferred_element_type=F32).astype(BF16)


def chunk_rows(chunk):
    return pl.ds(pl.multiple_of(chunk * 16, 16), 16)


def send_all(axis, size, me, source, target, send, recv):
    def step(offset, carry):
        peer = lax.rem(me + offset, size)
        pltpu.make_async_remote_copy(
            source(peer), target, send, recv, device_id={axis: peer}, device_id_type=MESH
        ).start()
        return carry

    lax.fori_loop(1, size, step, 0)


def wait_recv(view, recv):
    pltpu.make_async_copy(view, view, recv).wait()


def greet(axis, size, me, barrier):
    def step(index, carry):
        ahead = size // 2 + jnp.where(lax.rem(index, 2) == 1, -((index + 1) // 2), index // 2)
        pl.semaphore_signal(
            barrier, inc=1, device_id={axis: lax.rem(me + ahead, size)}, device_id_type=MESH
        )
        return carry

    lax.fori_loop(0, size - 1, step, 0)


def send_planes(plane, terms, others, rows, send, recv):
    chip, core = plane // 2, lax.rem(plane, 2)
    for ahead, other in ((2, 0), (2, 1), (1, 0), (3, 0), (1, 1), (3, 1), (0, 1)):
        peer = lax.rem(chip + ahead, 4) * 2 + lax.rem(core + other, 2)
        pltpu.make_async_remote_copy(
            terms.at[peer, :, rows],
            others.at[plane, :, rows],
            send,
            recv,
            device_id={"plane": peer},
            device_id_type=MESH,
        ).start()


def whole_kernel(
    w_ref,
    owner_in,
    counts_in,
    image_in,
    positions_in,
    weights_in,
    table_in,
    twiddle_in,
    others,
    owner,
    counts,
    image,
    positions,
    weights,
    table,
    twiddle,
    packed,
    kept,
    got_packed,
    got_kept,
    stacked,
    blocks,
    got,
    tiles,
    gridded,
    back,
    got_back,
    middle,
    screen,
    terms,
    all_taps,
    tile_weight,
    fields,
    names,
    seconds,
    local_sem,
    vis_send,
    vis_recv,
    out_send,
    out_recv,
    back_send,
    back_recv,
    term_send,
    term_recv,
):
    me = lax.axis_index("row")
    plane = lax.axis_index("plane")
    barrier = pltpu.get_barrier_semaphore()
    greet("row", ROWS, me, barrier)
    greet("plane", PLANES, plane, barrier)
    loads = [
        pltpu.make_async_copy(source, target, local_sem.at[index])
        for index, (source, target) in enumerate(
            (
                (owner_in, owner),
                (counts_in, counts),
                (image_in, image),
                (twiddle_in, twiddle),
                (positions_in, positions),
                (weights_in, weights),
                (table_in, table),
            )
        )
    ]
    for copy in loads:
        copy.start()
    w = w_ref[0]

    def load(block, rows, half):
        pairs = []
        for a in range(8):
            col = 256 * a + 128 * half
            cosine, sine = screen[0, rows, col : col + 128], screen[1, rows, col : col + 128]
            real, imag = image[0, rows, col : col + 128], image[1, rows, col : col + 128]
            pairs.append((real * cosine + imag * sine, real * sine - imag * cosine))
        return pairs

    def prepare(block, carry):
        rows = chunk_rows(block)
        for piece in range(16):
            lanes = slice(128 * piece, 128 * piece + 128)
            cosine, sine = chunk_screen(w, me * 64 + block * 16, 128 * piece)
            screen[0, rows, lanes] = cosine
            screen[1, rows, lanes] = sine
        return carry

    lax.fori_loop(0, 4, prepare, 0)
    for copy in loads[0:6]:
        copy.wait()
    place_of = lax.broadcasted_iota(jnp.int32, (1, V), 1)
    for peer in range(ROWS):
        pair = slice(2 * peer, 2 * peer + 2)
        packed[peer] = positions[0, 0, pair, :] * 8192 + positions[0, 1, pair, :]
        chosen = []
        for item in range(2):
            slot = 2 * peer + item
            chosen.append(jnp.where(place_of < counts[0, slot], weights[0, slot : slot + 1, :], 0.0))
        kept[peer] = jnp.concatenate(chosen, axis=0).astype(BF16)

    def first_spread(block, carry):
        spread_block(load, block, twiddle, stacked)
        return carry

    lax.fori_loop(0, 4, first_spread, 0)
    pl.semaphore_wait(barrier, ROWS + PLANES - 2)
    send_all("row", ROWS, me, lambda peer: packed.at[peer], got_packed.at[me], vis_send.at[0], vis_recv.at[0])
    loads[6].wait()
    turn_blocks(stacked, table, blocks)

    def send_chunk(chunk, carry):
        rows = chunk_rows(chunk)
        send_all(
            "row", ROWS, me, lambda peer: blocks.at[peer, rows], got.at[me, rows], out_send.at[chunk], out_recv.at[chunk]
        )
        return carry

    lax.fori_loop(0, 4, send_chunk, 0)
    send_all("row", ROWS, me, lambda peer: kept.at[peer], got_kept.at[me], vis_send.at[1], vis_recv.at[1])
    got_packed[me] = packed[me]
    got_kept[me] = kept[me]
    got[me] = blocks[me]
    places = place_index()
    most = pl.ds(0, ROWS - 1)
    wait_recv(got_packed.at[most], vis_recv.at[0])

    def tap_step(item, carry):
        name = owner[me * ROWS + item]

        def count(other, total):
            return total + jnp.where((owner[me * ROWS + other] == name) & (other < item), 1, 0)

        second = lax.fori_loop(0, ROWS, count, 0, unroll=True) > 0
        names[item] = name
        seconds[item] = jnp.where(second, 1, 0)
        both = got_packed[name]
        place = jnp.where(second, both[1:2], both[0:1])
        u_part = place // 8192
        all_taps[item, 0] = taps_of(u_part.astype(F32) * (1.0 / OVER), places).astype(BF16)
        all_taps[item, 1] = taps_of((place - u_part * 8192).astype(F32) * (1.0 / OVER), places).astype(BF16)
        return carry

    lax.fori_loop(0, ROWS, tap_step, 0)
    load_got = load_received(got)

    def second_spread(chunk, carry):
        wait_recv(got.at[most, chunk_rows(chunk)], out_recv.at[chunk])
        spread_block(load_got, chunk, twiddle, stacked)
        return carry

    lax.fori_loop(0, 4, second_spread, 0)
    turn_blocks(stacked, table, tiles)

    wait_recv(got_kept.at[most], vis_recv.at[1])
    for group in range(0, ROWS, 8):
        pairs = [got_kept[names[item]].astype(F32) for item in range(group, group + 8)]
        picked = [jnp.where(seconds[group + item] > 0, pairs[item][1:2], pairs[item][0:1]) for item in range(8)]
        for item in range(8):
            tile_weight[group + item] = picked[item]

    def grid_step(group, carry):
        for place in range(16):
            item = group * 16 + place
            gridded[item] = grid_tile(
                tiles[item], all_taps[item, 0], all_taps[item, 1].astype(F32), tile_weight[item]
            )
        return carry

    lax.fori_loop(0, 2, grid_step, 0)
    for pair in range(4):
        gather_pair(pair, gridded, table, twiddle, middle)
    emit_back = emit_fields(fields)
    for block in range(4):
        last_block(block, middle, emit_back)
    shuffle_fields(fields, back)

    def back_send_one(peer, chunk):
        pltpu.make_async_remote_copy(
            back.at[chunk, peer],
            got_back.at[chunk, me],
            back_send.at[chunk],
            back_recv.at[chunk],
            device_id={"row": peer},
            device_id_type=MESH,
        ).start()

    for first, second, middle_z, late in ((((0, 1), (0,), (0,), ()), ((2, 3), (1, 2), (1,), (0,)), ((), (3,), (2, 3), (1, 2)), ((), (), (), (3,)))):

        def back_step(offset, carry, first=first, second=second, middle_z=middle_z, late=late):
            peer = lax.rem(me + offset, ROWS)
            for chunks, chosen in (
                (first, peer < 4),
                (second, (peer >= 4) & (peer < 8)),
                (middle_z, (peer >= 8) & (peer < 16)),
                (late, peer >= 16),
            ):
                if chunks:

                    @pl.when(chosen)
                    def _(chunks=chunks):
                        for chunk in chunks:
                            back_send_one(peer, chunk)

            return carry

        lax.fori_loop(1, ROWS, back_step, 0)
    for chunk in range(4):
        got_back[chunk, me] = back[chunk, me]

    def emit(block, rows, half, re, im):
        for a in range(8):
            lanes = slice(128 * half, 128 * half + 128)
            full = slice(256 * a + 128 * half, 256 * a + 128 * half + 128)
            cosine, sine = screen[0, rows, full], screen[1, rows, full]
            terms[a, 0, rows, lanes] = (re[a] * cosine - im[a] * sine).astype(BF16)
            terms[a, 1, rows, lanes] = (re[a] * sine + im[a] * cosine).astype(BF16)

    def term_chunk(chunk, carry):
        wait_recv(got_back.at[chunk, most], back_recv.at[chunk])
        gather_chunk(chunk, got_back, table, twiddle, middle)
        last_block(chunk, middle, emit)
        rows = chunk_rows(chunk)
        send_planes(plane, terms, others, rows, term_send, term_recv)
        return carry

    lax.fori_loop(0, 4, term_chunk, 0)
    mine = pltpu.make_async_copy(terms.at[plane], others.at[plane], local_sem.at[0])
    mine.start()
    wait_recv(packed.at[most], vis_send.at[0])
    wait_recv(kept.at[most], vis_send.at[1])
    for chunk in range(4):
        wait_recv(blocks.at[most, chunk_rows(chunk)], out_send.at[chunk])
        wait_recv(back.at[chunk, most], back_send.at[chunk])
    mine.wait()
    rest = pl.ds(0, PLANES - 1)
    wait_recv(terms.at[rest], term_send)
    wait_recv(others.at[rest], term_recv)


def local(image, w_planes, owner, positions, weights, counts):
    table, twiddle = host_tables()
    smem = pl.BlockSpec(memory_space=pltpu.SMEM)
    anywhere = pl.BlockSpec(memory_space=pl.ANY)
    dma = pltpu.SemaphoreType.DMA
    block = pltpu.VMEM((ROWS, TILE, 128), BF16)
    others = pl.pallas_call(
        whole_kernel,
        out_shape=jax.ShapeDtypeStruct((PLANES, 2, 64, 256), BF16),
        in_specs=[smem] + [pl.BlockSpec(memory_space=pltpu.HBM)] * 7,
        out_specs=anywhere,
        scratch_shapes=[
            pltpu.SMEM((ROWS * ROWS,), jnp.int32),
            pltpu.SMEM((1, 64), jnp.int32),
            pltpu.VMEM((2, 64, EXTENT), F32),
            pltpu.VMEM((1, 2, 64, V), jnp.int32),
            pltpu.VMEM((1, 64, V), F32),
            pltpu.VMEM((512, 512), BF16),
            pltpu.VMEM((2, 8, 256), F32),
            pltpu.VMEM((ROWS, 2, V), jnp.int32),
            pltpu.VMEM((ROWS, 2, V), BF16),
            pltpu.VMEM((ROWS, 2, V), jnp.int32),
            pltpu.VMEM((ROWS, 2, V), BF16),
            pltpu.VMEM((8, 64, 512), BF16),
            block,
            block,
            block,
            block,
            pltpu.VMEM((4, ROWS, 16, 128), BF16),
            pltpu.VMEM((4, ROWS, 16, 128), BF16),
            pltpu.VMEM((8, 64, 512), F32),
            pltpu.VMEM((2, 64, EXTENT), F32),
            pltpu.VMEM((PLANES, 2, 64, 256), BF16),
            pltpu.VMEM((ROWS, 2, TILE, V), BF16),
            pltpu.VMEM((ROWS, 1, V), F32),
            pltpu.VMEM((16, 2, 64, 128), BF16),
            pltpu.SMEM((ROWS,), jnp.int32),
            pltpu.SMEM((ROWS,), jnp.int32),
            dma((7,)),
            dma((2,)),
            dma((2,)),
            dma((4,)),
            dma((4,)),
            dma((4,)),
            dma((4,)),
            dma,
            dma,
        ],
        compiler_params=pltpu.CompilerParams(collective_id=0, has_side_effects=True, vmem_limit_bytes=24 * 1024 * 1024),
        name="whole",
    )(
        w_planes,
        *[
            pltpu.with_memory_space_constraint(value, pltpu.HBM)
            for value in (
                owner.reshape(-1),
                counts,
                image,
                positions,
                weights,
                jnp.asarray(table),
                jnp.asarray(twiddle),
            )
        ],
    )
    return jnp.sum(others.astype(F32), axis=0)


def solution(mesh):
    in_specs = (
        P(None, "row", None),
        P("plane"),
        P("plane", None, None),
        P("plane", None, "row", None),
        P("plane", "row", None),
        P("plane", "row"),
    )
    out_specs = P(None, "row", "plane")
    return jax.shard_map(local, mesh=mesh, in_specs=in_specs, out_specs=out_specs, check_vma=False)
```
